32 devices in a mesh: date: 4 (over y, x), pix: 4 (over z), tile: 2 (over core).
Axes of the slice: x: 2, y: 2, z: 4, core: 2. Of those that a mesh axis runs over, the one named last changes fastest.
Arguments:
- reflectance: float32 [32, 7, 65536], P('date', None, ('tile', 'pix')), parts along dimension 2, may hold values from -6 to 6
- validity: int32 [32, 65536], P('date', ('tile', 'pix')), parts along dimension 1, may hold values from 0 to 1, as said below
- day_number: int32 [32], P('date'), may hold values from 1 to 63, as said below
Outputs:
- filled: float32 [32, 7, 65536], P('date', None, ('tile', 'pix')), parts along dimension 2
The draws below stay inside these ranges and needn't reach their ends.
There are 2 independent parts, one for each index of `tile`. The reference program is written for one: setup_inputs(seed, part) draws one part's arguments, and reference() takes and returns one part's arrays. A program takes and returns all parts, laid end to end along the dimension named above; an argument that names none is the same for every part. Nothing has to cross between parts.
Inputs may be any that keep to these rules, and one draw needn't show every extreme that they name: `validity`: 1 marks a usable observation, 0 a rejected one. `day_number`: strictly increasing along the dates, by 1 to 3 days from one date to the next, starting at day 1.
All inputs are finite; a program needn't handle non-finite values.
Results may differ from the reference program's by a relative error of at most 0.0003.
Values sent between devices are 32-bit elements; how exact they have to be, the bound alone decides.
No kernel may reach another device: no remote copies, remote signals or barrier semaphores. Data moves between devices by JAX's collectives and lax.ppermute only.
A program may use at most 64 MiB of HBM per device.

```python
import jax
import jax.numpy as jnp
from jax import lax

BANDS = 7
DATE_DEV = 8
DATES = 32
PIXELS = 32768


def draw_validity(key, part):
    picks = jax.random.randint(jax.random.fold_in(key, 11), (DATES, PIXELS), 0, 2 * DATE_DEV)
    kinds = jax.random.randint(jax.random.fold_in(key, 13), (PIXELS,), 0, 64)
    early = jax.random.randint(jax.random.fold_in(key, 17), (PIXELS,), 0, DATE_DEV)
    late = DATES - 1 - jax.random.randint(jax.random.fold_in(key, 19), (PIXELS,), 0, DATE_DEV)
    lonely = jax.random.randint(jax.random.fold_in(key, 29), (PIXELS,), 0, DATES)
    rows = lax.broadcasted_iota(jnp.int32, (DATES, PIXELS), 0)
    common = picks < 2
    at_ends = (rows == early[None, :]) | (rows == late[None, :])
    single = rows == lonely[None, :]
    kind_row = kinds[None, :]
    live = jnp.where(kind_row == 0, False, jnp.where(kind_row <= 2, at_ends, jnp.where(kind_row == 3, single, common)))
    return live.astype(jnp.int32)


def draw_day_number(key, part):
    picks = jax.random.randint(jax.random.fold_in(key, 23), (DATES,), 1, 4).astype(jnp.int32)
    before = jnp.roll(picks, 1)
    order = lax.broadcasted_iota(jnp.int32, (DATES,), 0)
    odd_step = jnp.where(order == DATES - 1, 2, picks)
    steps = jnp.where(order == 0, 1, jnp.where(order % 2 == 1, odd_step, 4 - before))
    return jnp.cumsum(steps).astype(jnp.int32)


def block_scale(own_key, extent, cuts, least, top_value):
    gain = 1.0
    for dim, parts in cuts:
        steps = jax.random.uniform(jax.random.fold_in(jax.random.fold_in(own_key, 6), dim), (parts,), jnp.float32, least / len(cuts), top_value / len(cuts))
        gain = gain * jnp.repeat(jnp.exp(steps), extent[dim] // parts).reshape((-1,) + (1,) * (len(extent) - 1 - dim))
    return gain


def scatter_about(own_key, dims, scale, bound, shards=(), dtype=jnp.bfloat16):
    array = scale * jax.random.normal(own_key, dims, jnp.float32)
    if shards:
        array = array * block_scale(own_key, dims, shards, -0.22, 0.18)
    return jnp.clip(array, -bound, bound).astype(dtype)


def setup_inputs(seed: int = 0, part: int = 0) -> dict:
    arg_keys = jax.random.split(jax.random.key(seed), 4)
    part_keys = jax.random.split(jax.random.fold_in(arg_keys[3], part), 4)
    return {
        "reflectance": scatter_about(part_keys[0], (DATES, BANDS, PIXELS), 1.0, 6.0, ((0, 4), (2, 4)), jnp.float32),
        "validity": draw_validity(jax.random.fold_in(jax.random.fold_in(arg_keys[3], part), 71), part),
        "day_number": draw_day_number(jax.random.fold_in(arg_keys[3], 71), part),
    }


far_day = 1073741824


def scan_block(values, validity, days):
    count = values.shape[0]
    live = validity > 0
    order = lax.broadcasted_iota(jnp.int32, validity.shape, 0)
    fwd_pos = lax.cummax(jnp.where(live, order, -1), axis=0)
    bwd_pos = lax.cummin(jnp.where(live, order, count), axis=0, reverse=True)
    fwd_val = jnp.take_along_axis(values, jnp.clip(fwd_pos, 0, count - 1)[:, None, :], axis=0)
    bwd_val = jnp.take_along_axis(values, jnp.clip(bwd_pos, 0, count - 1)[:, None, :], axis=0)
    day_col = jnp.broadcast_to(days[:, None], validity.shape).astype(jnp.int32)
    fwd_day = lax.cummax(jnp.where(live, day_col, -1), axis=0)
    bwd_day = lax.cummin(jnp.where(live, day_col, far_day), axis=0, reverse=True)
    return live, day_col, fwd_day, fwd_val, bwd_day, bwd_val


def blend(values, live, day_col, fwd_day, fwd_val, bwd_day, bwd_val):
    has_prev = fwd_day >= 0
    has_next = bwd_day < far_day
    inside = has_prev & has_next & jnp.logical_not(live)
    span = jnp.where(inside, bwd_day - fwd_day, 1).astype(jnp.float32)
    weight = (day_col - fwd_day).astype(jnp.float32) / span
    middle = fwd_val + weight[:, None, :] * (bwd_val - fwd_val)
    one_side = jnp.where(has_prev[:, None, :], fwd_val,
                         jnp.where(has_next[:, None, :], bwd_val, jnp.zeros_like(fwd_val)))
    chosen = jnp.where(inside[:, None, :], middle, one_side)
    return jnp.where(live[:, None, :], values, chosen)


def reference(reflectance, validity, day_number):
    live, day_col, fwd_day, fwd_val, bwd_day, bwd_val = scan_block(reflectance, validity, day_number)
    return blend(reflectance, live, day_col, fwd_day, fwd_val, bwd_day, bwd_val)
```

```python
import functools

import jax
import jax.numpy as jnp
from jax import lax
from jax.experimental import pallas as pl
from jax.experimental.pallas import tpu as pltpu
from jax.sharding import PartitionSpec as P

far_day = 1073741824.0
LANES = 128


def day_column(days_ref, count):
    rows = lax.broadcasted_iota(jnp.int32, (count, LANES), 0)
    col = jnp.zeros((count, LANES), jnp.float32)
    for t in range(count):
        col = jnp.where(rows == t, days_ref[t].astype(jnp.float32), col)
    return rows, col


def pick(x, pos):
    return jnp.take_along_axis(x, pos, axis=0)


def running(pos, rows, count, forward):
    step = 1
    while step < count:
        shift = step if forward else count - step
        moved = pltpu.roll(pos, shift, 0)
        if forward:
            pos = jnp.maximum(pos, jnp.where(rows >= step, moved, -1))
        else:
            pos = jnp.minimum(pos, jnp.where(rows < count - step, moved, count))
        step *= 2
    return pos


def whole(pos, count, last):
    step = 1
    while step < count:
        moved = pltpu.roll(pos, step, 0)
        pos = jnp.maximum(pos, moved) if last else jnp.minimum(pos, moved)
        step *= 2
    return pos


def summary_kernel(tops, me_ref, days_ref, refl_ref, valid_ref, *out_refs):
    bands, count, width = refl_ref.shape
    rows, day_col = day_column(days_ref, count)
    out_rows = lax.broadcasted_iota(jnp.int32, (bands + 1, LANES), 0)
    me = me_ref[0]
    wants_last = [lax.rem(lax.div(me, 1 << t), 2) == 0 for t in tops]
    for i in range(width // LANES):
        cols = pl.ds(i * LANES, LANES)
        live = valid_ref[:, cols] > 0
        last = whole(jnp.where(live, rows, -1), count, True)
        first = whole(jnp.where(live, rows, count), count, False)
        found = last >= 0
        for t, out_ref in zip(wants_last, out_refs):
            pos = jnp.where(found, jnp.where(t, last, first), 0)
            got = jnp.where(found, pick(day_col, pos), 0.0)
            for b in range(bands):
                got = jnp.where(out_rows == b, pick(refl_ref[b, :, cols], pos), got)
            out_ref[:, cols] = got


def fill_kernel(tops, me_ref, days_ref, refl_ref, valid_ref, *refs):
    got_refs, out_ref = refs[:-1], refs[-1]
    bands, count, width = refl_ref.shape
    rows, day_col = day_column(days_ref, count)
    me = me_ref[0]
    is_prev = [lax.rem(lax.div(me, 1 << t), 2) == 1 for t in tops]
    shape = (bands + 1, LANES)
    for i in range(width // LANES):
        cols = pl.ds(i * LANES, LANES)
        live = valid_ref[:, cols] > 0
        prev_pos = running(jnp.where(live, rows, -1), rows, count, True)
        next_pos = running(jnp.where(live, rows, count), rows, count, False)
        prev_in = prev_pos >= 0
        next_in = next_pos < count
        prev_pos = jnp.maximum(prev_pos, 0)
        next_pos = jnp.minimum(next_pos, count - 1)
        before = jnp.zeros(shape, jnp.float32)
        after = jnp.zeros(shape, jnp.float32)
        before_day = jnp.zeros(shape, jnp.float32)
        after_day = jnp.full(shape, far_day, jnp.float32)
        for earlier, got_ref in zip(is_prev, got_refs):
            got = got_ref[:, cols]
            day = jnp.broadcast_to(got[bands:], shape)
            day_p = jnp.where(earlier, day, 0.0)
            day_n = jnp.where(jnp.logical_or(earlier, day <= 0.0), far_day, day)
            before = jnp.where(day_p > before_day, got, before)
            after = jnp.where(day_n < after_day, got, after)
            before_day = jnp.maximum(before_day, day_p)
            after_day = jnp.minimum(after_day, day_n)
        prev_day = jnp.where(prev_in, pick(day_col, prev_pos), before_day[:1])
        next_day = jnp.where(next_in, pick(day_col, next_pos), after_day[:1])
        has_prev = prev_day > 0.0
        has_next = next_day < far_day
        both = jnp.logical_and(has_prev, has_next)
        span = jnp.maximum(jnp.where(both, next_day - prev_day, 1.0), 1.0)
        weight = jnp.where(
            both, (day_col - prev_day) / span, jnp.where(has_prev, 0.0, 1.0)
        )
        for b in range(bands):
            x = refl_ref[b, :, cols]
            prev = jnp.where(prev_in, pick(x, prev_pos), before[b : b + 1])
            nxt = jnp.where(next_in, pick(x, next_pos), after[b : b + 1])
            out_ref[b, :, cols] = prev + weight * (nxt - prev)


def body(devices, width, reflectance, validity, day_number):
    count, bands, pixels = reflectance.shape
    refl = jnp.transpose(reflectance, (1, 0, 2))
    me = lax.axis_index("date")
    me_arr = me.reshape(1).astype(jnp.int32)
    bits = devices.bit_length() - 1
    smem = pl.BlockSpec(memory_space=pltpu.SMEM)
    stack = pl.BlockSpec((bands, count, width), lambda i: (0, 0, i))
    flat = pl.BlockSpec((count, width), lambda i: (0, i))
    packet = pl.BlockSpec((bands + 1, width), lambda i: (0, i))
    params = pltpu.CompilerParams(vmem_limit_bytes=24 << 20)
    sends = pl.pallas_call(
        functools.partial(summary_kernel, list(range(bits))),
        grid=(pixels // width,),
        in_specs=[smem, smem, stack, flat],
        out_specs=[packet] * bits,
        out_shape=[jax.ShapeDtypeStruct((bands + 1, pixels), jnp.float32)] * bits,
        compiler_params=params,
        name="summary",
    )(me_arr, day_number, refl, validity)
    gots, tops = [], []
    for k in range(1, devices):
        top = k.bit_length() - 1
        pairs = [(d, d ^ k) for d in range(devices)]
        gots.append(lax.ppermute(sends[top], "date", pairs))
        tops.append(top)
    out = pl.pallas_call(
        functools.partial(fill_kernel, tops),
        grid=(pixels // width,),
        in_specs=[smem, smem, stack, flat] + [packet] * len(gots),
        out_specs=stack,
        out_shape=jax.ShapeDtypeStruct((bands, count, pixels), jnp.float32),
        compiler_params=params,
        name="fill",
    )(me_arr, day_number, refl, validity, *gots)
    return jnp.transpose(out, (1, 0, 2))


def solution(mesh):
    placed = (P("date", None, ("tile", "pix")), P("date", ("tile", "pix")), P("date"))
    return jax.shard_map(
        functools.partial(body, mesh.shape["date"], 1024),
        mesh=mesh,
        in_specs=placed,
        out_specs=P("date", None, ("tile", "pix")),
        check_vma=False,
    )
```

```python
import functools

import jax
import jax.numpy as jnp
from jax import lax
from jax.experimental import pallas as pl
from jax.experimental.pallas import tpu as pltpu
from jax.sharding import PartitionSpec as P

LANES = 128
TOP = 1048576.0
VMEM = pl.BlockSpec(memory_space=pltpu.VMEM)
HBM = pl.BlockSpec(memory_space=pltpu.HBM)
PARAMS = pltpu.CompilerParams(vmem_limit_bytes=16 << 20)


def f32(*shape):
    return jax.ShapeDtypeStruct(shape, jnp.float32)


def pick(x, pos):
    return jnp.take_along_axis(x, pos, axis=0, mode="promise_in_bounds")


def sublane_max(x, count):
    step = 1
    while step < count:
        x = jnp.maximum(x, pltpu.roll(x, step, 0))
        step *= 2
    return x


def running(pos, rows, count, forward):
    step = 1
    while step < count:
        if forward:
            moved = pltpu.roll(pos, step, 0)
            pos = jnp.maximum(pos, jnp.where(rows >= step, moved, -1))
        else:
            moved = pltpu.roll(pos, count - step, 0)
            pos = jnp.minimum(pos, jnp.where(rows < count - step, moved, count))
        step *= 2
    return pos


def span_of(i):
    return pl.ds(pl.multiple_of(i * LANES, LANES), LANES)


def packet_of(values, live, day_col, rows, packet_rows, firsts):
    count = rows.shape[0]
    bands = len(values)
    outs = []
    for first in firsts:
        order = jnp.where(first, count - rows, rows + 1)
        best = sublane_max(jnp.where(live, order, 0), count)
        pos = jnp.where(first, count - best, best - 1) & (count - 1)
        near = jnp.where(first, TOP - day_col, day_col)
        got = pick(near, pos)
        for b in range(bands):
            got = jnp.where(packet_rows == b, pick(values[b], pos), got)
        outs.append(jnp.where(best > 0, got, 0.0))
    return outs


def bit_of(me, t):
    return lax.rem(lax.div(me, 1 << t), 2) == 1


def flags():
    me = lax.axis_index("date")
    return bit_of(me, 0), bit_of(me, 1), jnp.logical_or(me == 1, me == 2)


def tile_rows(bands, count):
    rows = lax.broadcasted_iota(jnp.int32, (count, LANES), 0)
    packet_rows = lax.broadcasted_iota(jnp.int32, (bands + 1, LANES), 0)
    return rows, packet_rows


def load_kernel(piece, bits, days_in, refl_in, valid_in, refl, valid, day_out, *rest):
    sends, (days, day_sem, sems) = rest[: len(bits)], rest[len(bits) :]
    bands, count, pixels = refl.shape
    half = sends[0].shape[1]
    day_copy = pltpu.make_async_copy(days_in, days, day_sem)
    day_copy.start()
    copies = []
    at = 0
    while at < pixels:
        width = piece if at < half else pixels - half
        cols = pl.ds(at, width)
        k = len(copies)
        pair = (
            pltpu.make_async_copy(
                valid_in.at[:, cols], valid.at[:, cols], sems.at[2 * k]
            ),
            pltpu.make_async_copy(
                refl_in.at[:, :, cols], refl.at[:, :, cols], sems.at[2 * k + 1]
            ),
        )
        for c in pair:
            c.start()
        copies.append(pair)
        at += width
    rows, packet_rows = tile_rows(bands, count)
    me = lax.axis_index("date")
    firsts = [bit_of(me, t) for t in bits]
    day_copy.wait()
    day_col = jnp.zeros((count, LANES), jnp.float32)
    for t in range(count):
        day_col = jnp.where(rows == t, days[t].astype(jnp.float32), day_col)
    day_out[...] = day_col
    for k in range(half // piece):
        for c in copies[k]:
            c.wait()

        @pl.loop(0, piece // LANES // 4)
        def _(j):
            for u in range(4):
                cols = span_of(k * (piece // LANES) + j * 4 + u)
                live = valid[:, cols] > 0
                values = [refl[b, :, cols] for b in range(bands)]
                packets = packet_of(values, live, day_col, rows, packet_rows, firsts)
                for send, packet in zip(sends, packets):
                    send[:, cols] = packet

    for pair in copies[half // piece :]:
        for c in pair:
            c.wait()


def second_kernel(refl, valid, day_in, sx_first, sy, sx, side):
    bands, count, pixels = refl.shape
    half = pixels // 2
    rows, packet_rows = tile_rows(bands, count)
    odd, upper, inner = flags()
    day_col = day_in[...]

    @pl.loop(0, half // LANES // 4)
    def _(j):
        for u in range(4):
            cols = span_of(j * 4 + u)
            far = span_of(half // LANES + j * 4 + u)
            live = valid[:, far] > 0
            values = [refl[b, :, far] for b in range(bands)]
            a, b = packet_of(values, live, day_col, rows, packet_rows, (upper, odd))
            sy[:, cols] = a
            sx[:, cols] = b
            side[:, cols] = jnp.where(inner, sx_first[:, cols], b)


def nearness(packet):
    return jnp.broadcast_to(packet[packet.shape[0] - 1 :], packet.shape)


def join_near_kernel(own, got, out):
    @pl.loop(0, own.shape[1] // LANES // 4)
    def _(j):
        for u in range(4):
            cols = span_of(j * 4 + u)
            a, b = own[:, cols], got[:, cols]
            out[:, cols] = jnp.where(nearness(a) >= nearness(b), a, b)


def join_own_kernel(own, got, out):
    _, _, inner = flags()

    @pl.loop(0, own.shape[1] // LANES // 4)
    def _(j):
        for u in range(4):
            cols = span_of(j * 4 + u)
            a, b = own[:, cols], got[:, cols]
            use = jnp.logical_and(inner, nearness(a) > 0.0)
            out[:, cols] = jnp.where(use, a, b)


def merge_first(refs, cols):
    _, upper, inner = flags()
    main, side, other = (r[:, cols] for r in refs)
    side = jnp.where(inner, 0.0, side)
    other = jnp.where(inner, other, 0.0)
    near = jnp.where(nearness(main) >= nearness(side), main, side)
    return jnp.where(upper, near, other), jnp.where(upper, other, near)


def merge_second(refs, cols):
    _, upper, inner = flags()
    main, more, side = (r[:, cols] for r in refs)
    other = jnp.where(inner, side, 0.0)
    near = jnp.where(nearness(main) >= nearness(more), main, more)
    return jnp.where(upper, near, other), jnp.where(upper, other, near)


def merge_all(bits, refs, cols):
    me = lax.axis_index("date")
    before = jnp.zeros((refs[0].shape[0], LANES), jnp.float32)
    after = before
    for t, ref in zip(bits, refs):
        got = ref[:, cols]
        prev = jnp.where(bit_of(me, t), got, 0.0)
        nxt = jnp.where(bit_of(me, t), 0.0, got)
        before = jnp.where(nearness(prev) > nearness(before), prev, before)
        after = jnp.where(nearness(nxt) > nearness(after), nxt, after)
    return before, after


def fill_kernel(start, width, piece, packets, merge, refl, valid, day_in, *rest):
    gots = rest[:packets]
    out, buf, sems = rest[-3:]
    bands, count, _ = refl.shape
    rows, _ = tile_rows(bands, count)
    day_col = day_in[...]
    copies = []
    for k in range(width // piece):

        @pl.loop(0, piece // LANES // 4)
        def _(j):
            for u in range(4):
                i = k * (piece // LANES) + j * 4 + u
                cols = span_of(i)
                far = span_of(start // LANES + i)
                live = valid[:, far] > 0
                prev_pos = running(jnp.where(live, rows, -1), rows, count, True)
                next_pos = running(jnp.where(live, rows, count), rows, count, False)
                prev_in = prev_pos >= 0
                next_in = next_pos < count
                prev_pos = prev_pos & (count - 1)
                next_pos = next_pos & (count - 1)
                before, after = merge(gots, cols)
                prev_day = jnp.where(prev_in, pick(day_col, prev_pos), before[bands:])
                next_day = jnp.where(
                    next_in, pick(day_col, next_pos), TOP - after[bands:]
                )
                has_prev = prev_day > 0.0
                has_next = next_day < TOP
                both = jnp.logical_and(has_prev, has_next)
                span = jnp.maximum(jnp.where(both, next_day - prev_day, 1.0), 1.0)
                weight = jnp.where(
                    both, (day_col - prev_day) / span, jnp.where(has_prev, 0.0, 1.0)
                )
                for b in range(bands):
                    x = refl[b, :, far]
                    prev = jnp.where(prev_in, pick(x, prev_pos), before[b : b + 1])
                    nxt = jnp.where(next_in, pick(x, next_pos), after[b : b + 1])
                    buf[b, :, cols] = prev + weight * (nxt - prev)

        copy = pltpu.make_async_copy(
            buf.at[:, :, pl.ds(k * piece, piece)],
            out.at[:, :, pl.ds(start + k * piece, piece)],
            sems.at[k],
        )
        copy.start()
        copies.append(copy)
    for copy in copies:
        copy.wait()


def fill(name, start, piece, merge, refl, valid, day_col, gots, out=None):
    bands, count, pixels = refl.shape
    width = gots[0].shape[1]
    held = () if out is None else (out,)
    return pl.pallas_call(
        functools.partial(fill_kernel, start, width, piece, len(gots), merge),
        in_specs=[VMEM] * (3 + len(gots)) + [HBM] * len(held),
        out_specs=HBM,
        out_shape=f32(bands, count, pixels),
        input_output_aliases={} if out is None else {3 + len(gots): 0},
        scratch_shapes=[
            pltpu.VMEM((bands, count, width), jnp.float32),
            pltpu.SemaphoreType.DMA((width // piece,)),
        ],
        compiler_params=PARAMS,
        name=name,
    )(refl, valid, day_col, *gots, *held)


def load(piece, width, bits, days, stack, validity):
    bands, count, pixels = stack.shape
    args = (pltpu.with_memory_space_constraint(a, pltpu.HBM) for a in (days, stack, validity))
    return pl.pallas_call(
        functools.partial(load_kernel, piece, bits),
        in_specs=[HBM] * 3,
        out_specs=[VMEM] * (3 + len(bits)),
        out_shape=[
            f32(bands, count, pixels),
            jax.ShapeDtypeStruct((count, pixels), jnp.int32),
            f32(count, LANES),
        ]
        + [f32(bands + 1, width)] * len(bits),
        scratch_shapes=[
            pltpu.SMEM((count,), jnp.int32),
            pltpu.SemaphoreType.DMA,
            pltpu.SemaphoreType.DMA((2 * (width // piece + 1),)),
        ],
        compiler_params=PARAMS,
        name="load",
    )(*args)


def body_any(devices, reflectance, validity, day_number):
    pixels = reflectance.shape[2]
    piece = pixels // 8
    stack = jnp.transpose(reflectance, (1, 0, 2))
    bits = list(range((devices - 1).bit_length()))
    refl, valid, day_col, *sends = load(piece, pixels, bits, day_number, stack, validity)
    gots, tops = [], []
    for k in range(1, 1 << len(bits)):
        pairs = [(d, d ^ k) for d in range(devices) if d ^ k < devices]
        tops.append(k.bit_length() - 1)
        gots.append(lax.ppermute(sends[tops[-1]], "date", pairs))
    merge = functools.partial(merge_all, tops)
    out = fill("fill", 0, piece, merge, refl, valid, day_col, gots)
    return jnp.transpose(out, (1, 0, 2))


def body(reflectance, validity, day_number):
    count, bands, pixels = reflectance.shape
    half = pixels // 2
    piece = half // 4
    stack = jnp.transpose(reflectance, (1, 0, 2))
    packet = f32(bands + 1, half)
    across = lambda x: lax.ppermute(x, "date", [(d, d ^ 1) for d in range(4)])
    along = lambda x: lax.ppermute(x, "date", [(d, d ^ 2) for d in range(4)])

    refl, valid, day_col, sy1, sx1 = load(piece, half, (1, 0), day_number, stack, validity)
    got1 = across(sy1)
    sy2, sx2, side = pl.pallas_call(
        second_kernel,
        in_specs=[VMEM] * 4,
        out_specs=[VMEM] * 3,
        out_shape=[packet] * 3,
        compiler_params=PARAMS,
        name="second",
    )(refl, valid, day_col, sx1)
    got2 = along(sy2)
    side = across(side)
    join = dict(
        in_specs=[VMEM] * 2, out_specs=VMEM, out_shape=packet, compiler_params=PARAMS
    )
    joined1 = pl.pallas_call(join_near_kernel, name="join_first", **join)(sy1, got1)
    far1 = along(joined1)
    joined2 = pl.pallas_call(join_own_kernel, name="join_second", **join)(sx2, got2)
    far2 = across(joined2)
    arrays = (refl, valid, day_col)
    out = fill("fill_first", 0, piece, merge_first, *arrays, (far1, side, got1))
    out = fill("fill_second", half, piece, merge_second, *arrays, (got2, far2, side), out)
    return jnp.transpose(out, (1, 0, 2))


def solution(mesh):
    placed = (P("date", None, ("tile", "pix")), P("date", ("tile", "pix")), P("date"))
    devices = mesh.shape["date"]
    return jax.shard_map(
        body if devices == 4 else functools.partial(body_any, devices),
        mesh=mesh,
        in_specs=placed,
        out_specs=P("date", None, ("tile", "pix")),
        check_vma=False,
    )
```

```python
import functools

import jax
import jax.numpy as jnp
from jax import lax
from jax.experimental import pallas as pl
from jax.experimental.pallas import tpu as pltpu
from jax.sharding import PartitionSpec as P

LANES = 128
TOP = 1048576.0
VMEM = pl.BlockSpec(memory_space=pltpu.VMEM)
HBM = pl.BlockSpec(memory_space=pltpu.HBM)
PARAMS = pltpu.CompilerParams(vmem_limit_bytes=16 << 20)


def f32(*shape):
    return jax.ShapeDtypeStruct(shape, jnp.float32)


def pick(x, pos):
    return jnp.take_along_axis(x, pos, axis=0, mode="promise_in_bounds")


def sublane_max(x, count):
    step = 1
    while step < count:
        x = jnp.maximum(x, pltpu.roll(x, step, 0))
        step *= 2
    return x


def running(pos, rows, count, forward):
    step = 1
    while step < count:
        if forward:
            moved = pltpu.roll(pos, step, 0)
            pos = jnp.maximum(pos, jnp.where(rows >= step, moved, -1))
        else:
            moved = pltpu.roll(pos, count - step, 0)
            pos = jnp.minimum(pos, jnp.where(rows < count - step, moved, count))
        step *= 2
    return pos


def span_of(i):
    return pl.ds(pl.multiple_of(i * LANES, LANES), LANES)


def packet_of(values, live, day_col, rows, packet_rows, firsts):
    count = rows.shape[0]
    bands = len(values)
    outs = []
    for first in firsts:
        order = jnp.where(first, count - rows, rows + 1)
        best = sublane_max(jnp.where(live, order, 0), count)
        pos = jnp.where(first, count - best, best - 1) & (count - 1)
        near = jnp.where(first, TOP - day_col, day_col)
        got = pick(near, pos)
        for b in range(bands):
            got = jnp.where(packet_rows == b, pick(values[b], pos), got)
        outs.append(jnp.where(best > 0, got, 0.0))
    return outs


def bit_of(me, t):
    return lax.rem(lax.div(me, 1 << t), 2) == 1


def flags():
    me = lax.axis_index("date")
    return bit_of(me, 0), bit_of(me, 1), jnp.logical_or(me == 1, me == 2)


def tile_rows(bands, count):
    rows = lax.broadcasted_iota(jnp.int32, (count, LANES), 0)
    packet_rows = lax.broadcasted_iota(jnp.int32, (bands + 1, LANES), 0)
    return rows, packet_rows


def load_kernel(piece, bits, days_in, refl_in, valid_in, day_out, *rest):
    sends, (refl, valid, days, day_sem, sems) = rest[: len(bits)], rest[len(bits) :]
    bands, count, pixels = refl.shape
    half = sends[0].shape[1]
    day_copy = pltpu.make_async_copy(days_in, days, day_sem)
    day_copy.start()
    copies = []
    at = 0
    while at < half:
        width = piece
        cols = pl.ds(at, width)
        k = len(copies)
        pair = (
            pltpu.make_async_copy(
                valid_in.at[:, cols], valid.at[:, cols], sems.at[2 * k]
            ),
            pltpu.make_async_copy(
                refl_in.at[:, :, cols], refl.at[:, :, cols], sems.at[2 * k + 1]
            ),
        )
        for c in pair:
            c.start(priority=1)
        copies.append(pair)
        at += width
    rows, packet_rows = tile_rows(bands, count)
    me = lax.axis_index("date")
    firsts = [bit_of(me, t) for t in bits]
    day_copy.wait()
    day_col = jnp.zeros((count, LANES), jnp.float32)
    for t in range(count):
        day_col = jnp.where(rows == t, days[t].astype(jnp.float32), day_col)
    day_out[...] = day_col
    for k in range(half // piece):
        for c in copies[k]:
            c.wait()

        @pl.loop(0, piece // LANES // 4)
        def _(j):
            for u in range(4):
                cols = span_of(k * (piece // LANES) + j * 4 + u)
                live = valid[:, cols] > 0
                values = [refl[b, :, cols] for b in range(bands)]
                packets = packet_of(values, live, day_col, rows, packet_rows, firsts)
                for send, packet in zip(sends, packets):
                    send[:, cols] = packet


def second_kernel(refl, valid, day_in, sy, sx, side):
    bands, count, pixels = refl.shape
    half = pixels // 2
    rows, packet_rows = tile_rows(bands, count)
    odd, upper, inner = flags()
    day_col = day_in[...]

    @pl.loop(0, half // LANES // 4)
    def _(j):
        for u in range(4):
            cols = span_of(j * 4 + u)
            far = span_of(half // LANES + j * 4 + u)
            live = valid[:, far] > 0
            values = [refl[b, :, far] for b in range(bands)]
            a, b = packet_of(values, live, day_col, rows, packet_rows, (upper, odd))
            sy[:, cols] = a
            sx[:, cols] = b
            live = valid[:, cols] > 0
            values = [refl[k, :, cols] for k in range(bands)]
            (c,) = packet_of(values, live, day_col, rows, packet_rows, (odd,))
            side[:, cols] = jnp.where(inner, c, b)


def nearness(packet):
    return jnp.broadcast_to(packet[packet.shape[0] - 1 :], packet.shape)


def join_near_kernel(own, got, out):
    @pl.loop(0, own.shape[1] // LANES // 4)
    def _(j):
        for u in range(4):
            cols = span_of(j * 4 + u)
            a, b = own[:, cols], got[:, cols]
            out[:, cols] = jnp.where(nearness(a) >= nearness(b), a, b)


def join_own_kernel(own, got, out):
    _, _, inner = flags()

    @pl.loop(0, own.shape[1] // LANES // 4)
    def _(j):
        for u in range(4):
            cols = span_of(j * 4 + u)
            a, b = own[:, cols], got[:, cols]
            use = jnp.logical_and(inner, nearness(a) > 0.0)
            out[:, cols] = jnp.where(use, a, b)


def merge_first(refs, cols):
    _, upper, inner = flags()
    main, side, other = (r[:, cols] for r in refs)
    side = jnp.where(inner, 0.0, side)
    other = jnp.where(inner, other, 0.0)
    near = jnp.where(nearness(main) >= nearness(side), main, side)
    return jnp.where(upper, near, other), jnp.where(upper, other, near)


def merge_second(refs, cols):
    _, upper, inner = flags()
    main, more, side = (r[:, cols] for r in refs)
    other = jnp.where(inner, side, 0.0)
    near = jnp.where(nearness(main) >= nearness(more), main, more)
    return jnp.where(upper, near, other), jnp.where(upper, other, near)


def merge_all(bits, refs, cols):
    me = lax.axis_index("date")
    before = jnp.zeros((refs[0].shape[0], LANES), jnp.float32)
    after = before
    for t, ref in zip(bits, refs):
        got = ref[:, cols]
        prev = jnp.where(bit_of(me, t), got, 0.0)
        nxt = jnp.where(bit_of(me, t), 0.0, got)
        before = jnp.where(nearness(prev) > nearness(before), prev, before)
        after = jnp.where(nearness(nxt) > nearness(after), nxt, after)
    return before, after


def near_kernel(refl, valid, day_in, prev_out, next_out, prev_days, next_days):
    bands, count, pixels = refl.shape
    rows, _ = tile_rows(bands, count)
    day_col = day_in[...]

    @pl.loop(0, pixels // LANES // 4)
    def _(j):
        for u in range(4):
            cols = span_of(j * 4 + u)
            live = valid[:, cols] > 0
            prev_pos = running(jnp.where(live, rows, -1), rows, count, True)
            next_pos = running(jnp.where(live, rows, count), rows, count, False)
            prev_in = prev_pos >= 0
            next_in = next_pos < count
            prev_pos = prev_pos & (count - 1)
            next_pos = next_pos & (count - 1)
            prev_days[:, cols] = jnp.where(prev_in, pick(day_col, prev_pos), 0.0)
            next_days[:, cols] = jnp.where(next_in, pick(day_col, next_pos), TOP)
            for b in range(bands):
                x = refl[b, :, cols]
                prev_out[b, :, cols] = pick(x, prev_pos)
                next_out[b, :, cols] = pick(x, next_pos)


def fill_kernel(start, width, piece, packets, merge, *refs):
    prev_own, next_own, prev_days, next_days, day_in = refs[:5]
    gots = refs[5 : 5 + packets]
    out, buf, sems = refs[-3:]
    bands, count, _ = prev_own.shape
    day_col = day_in[...]
    copies = []
    for k in range(width // piece):

        @pl.loop(0, piece // LANES // 4)
        def _(j):
            for u in range(4):
                i = k * (piece // LANES) + j * 4 + u
                cols = span_of(i)
                far = span_of(start // LANES + i)
                before, after = merge(gots, cols)
                prev_day, next_day = prev_days[:, far], next_days[:, far]
                prev_in, next_in = prev_day > 0.0, next_day < TOP
                prev_day = jnp.where(prev_in, prev_day, before[bands:])
                next_day = jnp.where(next_in, next_day, TOP - after[bands:])
                has_prev = prev_day > 0.0
                both = jnp.logical_and(has_prev, next_day < TOP)
                span = jnp.maximum(jnp.where(both, next_day - prev_day, 1.0), 1.0)
                weight = jnp.where(
                    both, (day_col - prev_day) / span, jnp.where(has_prev, 0.0, 1.0)
                )
                for b in range(bands):
                    prev = jnp.where(prev_in, prev_own[b, :, far], before[b : b + 1])
                    nxt = jnp.where(next_in, next_own[b, :, far], after[b : b + 1])
                    buf[b, :, cols] = prev + weight * (nxt - prev)

        copy = pltpu.make_async_copy(
            buf.at[:, :, pl.ds(k * piece, piece)],
            out.at[:, :, pl.ds(start + k * piece, piece)],
            sems.at[k],
        )
        copy.start()
        copies.append(copy)
    for copy in copies:
        copy.wait()


def nearest(refl, valid, day_col):
    bands, count, pixels = refl.shape
    return pl.pallas_call(
        near_kernel,
        in_specs=[VMEM] * 3,
        out_specs=[VMEM] * 4,
        out_shape=[f32(bands, count, pixels)] * 2 + [f32(count, pixels)] * 2,
        compiler_params=PARAMS,
        name="nearest",
    )(refl, valid, day_col)


def fill(name, start, piece, merge, near, day_col, gots, out=None):
    bands, count, pixels = near[0].shape
    width = gots[0].shape[1]
    held = () if out is None else (out,)
    return pl.pallas_call(
        functools.partial(fill_kernel, start, width, piece, len(gots), merge),
        in_specs=[VMEM] * (5 + len(gots)) + [HBM] * len(held),
        out_specs=HBM,
        out_shape=f32(bands, count, pixels),
        input_output_aliases={} if out is None else {5 + len(gots): 0},
        scratch_shapes=[
            pltpu.VMEM((bands, count, width), jnp.float32),
            pltpu.SemaphoreType.DMA((width // piece,)),
        ],
        compiler_params=PARAMS,
        name=name,
    )(*near, day_col, *gots, *held)


def load(piece, width, bits, days, stack, validity):
    bands, count, pixels = stack.shape
    args = (pltpu.with_memory_space_constraint(a, pltpu.HBM) for a in (days, stack, validity))
    return pl.pallas_call(
        functools.partial(load_kernel, piece, bits),
        in_specs=[HBM] * 3,
        out_specs=[VMEM] * (1 + len(bits)),
        out_shape=[f32(count, LANES)] + [f32(bands + 1, width)] * len(bits),
        scratch_shapes=[
            pltpu.VMEM((bands, count, width), jnp.float32),
            pltpu.VMEM((count, width), jnp.int32),
            pltpu.SMEM((count,), jnp.int32),
            pltpu.SemaphoreType.DMA,
            pltpu.SemaphoreType.DMA((2 * (width // piece + 1),)),
        ],
        compiler_params=PARAMS,
        name="load",
    )(*args)


def body_any(devices, reflectance, validity, day_number):
    pixels = reflectance.shape[2]
    piece = pixels // 8
    stack = jnp.transpose(reflectance, (1, 0, 2))
    bits = list(range((devices - 1).bit_length()))
    day_col, *sends = load(piece, pixels, bits, day_number, stack, validity)
    refl, valid = stack, validity
    gots, tops = [], []
    for k in range(1, 1 << len(bits)):
        pairs = [(d, d ^ k) for d in range(devices) if d ^ k < devices]
        tops.append(k.bit_length() - 1)
        gots.append(lax.ppermute(sends[tops[-1]], "date", pairs))
    merge = functools.partial(merge_all, tops)
    out = fill("fill", 0, piece, merge, nearest(refl, valid, day_col), day_col, gots)
    return jnp.transpose(out, (1, 0, 2))


def body(reflectance, validity, day_number):
    count, bands, pixels = reflectance.shape
    half = pixels // 2
    piece = half // 4
    stack = jnp.transpose(reflectance, (1, 0, 2))
    packet = f32(bands + 1, half)
    across = lambda x: lax.ppermute(x, "date", [(d, d ^ 1) for d in range(4)])
    along = lambda x: lax.ppermute(x, "date", [(d, d ^ 2) for d in range(4)])

    day_col, sy1 = load(piece, half, (1,), day_number, stack, validity)
    refl, valid = stack, validity
    got1 = across(sy1)
    sy2, sx2, side = pl.pallas_call(
        second_kernel,
        in_specs=[VMEM] * 3,
        out_specs=[VMEM] * 3,
        out_shape=[packet] * 3,
        compiler_params=PARAMS,
        name="second",
    )(refl, valid, day_col)
    got2 = along(sy2)
    side = across(side)
    join = dict(
        in_specs=[VMEM] * 2, out_specs=VMEM, out_shape=packet, compiler_params=PARAMS
    )
    joined1 = pl.pallas_call(join_near_kernel, name="join_first", **join)(sy1, got1)
    far1 = along(joined1)
    joined2 = pl.pallas_call(join_own_kernel, name="join_second", **join)(sx2, got2)
    far2 = across(joined2)
    arrays = (nearest(refl, valid, day_col), day_col)
    out = fill("fill_first", 0, piece, merge_first, *arrays, (far1, side, got1))
    out = fill("fill_second", half, piece, merge_second, *arrays, (got2, far2, side), out)
    return jnp.transpose(out, (1, 0, 2))


def solution(mesh):
    placed = (P("date", None, ("tile", "pix")), P("date", ("tile", "pix")), P("date"))
    devices = mesh.shape["date"]
    return jax.shard_map(
        body if devices == 4 else functools.partial(body_any, devices),
        mesh=mesh,
        in_specs=placed,
        out_specs=P("date", None, ("tile", "pix")),
        check_vma=False,
    )
```

```python
import functools

import jax
import jax.numpy as jnp
from jax import lax
from jax.experimental import pallas as pl
from jax.experimental.pallas import tpu as pltpu
from jax.sharding import PartitionSpec as P


LANES = 128
TOP = 1048576.0
VMEM = pl.BlockSpec(memory_space=pltpu.VMEM)
HBM = pl.BlockSpec(memory_space=pltpu.HBM)
PARAMS = pltpu.CompilerParams(vmem_limit_bytes=16 << 20)


def f32(*shape):
    return jax.ShapeDtypeStruct(shape, jnp.float32)


def pick(x, pos):
    return jnp.take_along_axis(x, pos, axis=0, mode="promise_in_bounds")


def sublane_max(x, count):
    step = 1
    while step < count:
        x = jnp.maximum(x, pltpu.roll(x, step, 0))
        step *= 2
    return x


def running(pos, rows, count, forward):
    step = 1
    while step < count:
        if forward:
            moved = pltpu.roll(pos, step, 0)
            pos = jnp.maximum(pos, jnp.where(rows >= step, moved, -1))
        else:
            moved = pltpu.roll(pos, count - step, 0)
            pos = jnp.minimum(pos, jnp.where(rows < count - step, moved, count))
        step *= 2
    return pos


def span_of(i):
    return pl.ds(pl.multiple_of(i * LANES, LANES), LANES)


def packet_of(values, live, day_col, rows, packet_rows, firsts):
    count = rows.shape[0]
    bands = len(values)
    outs = []
    for first in firsts:
        order = jnp.where(first, count - rows, rows + 1)
        best = sublane_max(jnp.where(live, order, 0), count)
        pos = jnp.where(first, count - best, best - 1) & (count - 1)
        near = jnp.where(first, TOP - day_col, day_col)
        got = pick(near, pos)
        for b in range(bands):
            got = jnp.where(packet_rows == b, pick(values[b], pos), got)
        outs.append(jnp.where(best > 0, got, 0.0))
    return outs


def bit_of(me, t):
    return lax.rem(lax.div(me, 1 << t), 2) == 1


def flags():
    me = lax.axis_index("date")
    return bit_of(me, 0), bit_of(me, 1), jnp.logical_or(me == 1, me == 2)


def tile_rows(bands, count):
    rows = lax.broadcasted_iota(jnp.int32, (count, LANES), 0)
    packet_rows = lax.broadcasted_iota(jnp.int32, (bands + 1, LANES), 0)
    return rows, packet_rows


def load_kernel(piece, bits, days_in, refl_in, valid_in, day_out, *rest):
    sends, (refl, valid, days, day_sem, sems) = rest[: len(bits)], rest[len(bits) :]
    bands, count, _ = refl.shape
    half = sends[0].shape[1]
    day_copy = pltpu.make_async_copy(days_in, days, day_sem)
    day_copy.start()
    copies = []
    at = 0
    while at < half:
        width = piece
        cols = pl.ds(at, width)
        k = len(copies)
        pair = (
            pltpu.make_async_copy(
                valid_in.at[:, cols], valid.at[:, cols], sems.at[2 * k]
            ),
            pltpu.make_async_copy(
                refl_in.at[:, :, cols], refl.at[:, :, cols], sems.at[2 * k + 1]
            ),
        )
        for c in pair:
            c.start(priority=1)
        copies.append(pair)
        at += width
    rows, packet_rows = tile_rows(bands, count)
    me = lax.axis_index("date")
    firsts = [bit_of(me, t) for t in bits]
    day_copy.wait()
    day_col = jnp.zeros((count, LANES), jnp.float32)
    for t in range(count):
        day_col = jnp.where(rows == t, days[t].astype(jnp.float32), day_col)
    day_out[...] = day_col
    for k in range(half // piece):
        for c in copies[k]:
            c.wait()

        @pl.loop(0, piece // LANES // 4)
        def _(j):
            for u in range(4):
                cols = span_of(k * (piece // LANES) + j * 4 + u)
                live = valid[:, cols] > 0
                values = [refl[b, :, cols] for b in range(bands)]
                packets = packet_of(values, live, day_col, rows, packet_rows, firsts)
                for send, packet in zip(sends, packets):
                    send[:, cols] = packet


def second_kernel(refl, valid, day_in, sy):
    bands, count, pixels = refl.shape
    half = pixels // 2
    rows, packet_rows = tile_rows(bands, count)
    _, upper, _ = flags()
    day_col = day_in[...]

    @pl.loop(0, half // LANES // 4)
    def _(j):
        for u in range(4):
            cols = span_of(j * 4 + u)
            far = span_of(half // LANES + j * 4 + u)
            live = valid[:, far] > 0
            values = [refl[k, :, far] for k in range(bands)]
            (a,) = packet_of(values, live, day_col, rows, packet_rows, (upper,))
            sy[:, cols] = a


def side_kernel(refl, valid, day_in, sx, side):
    bands, count, pixels = refl.shape
    half = pixels // 2
    rows, packet_rows = tile_rows(bands, count)
    odd, _, inner = flags()
    day_col = day_in[...]

    @pl.loop(0, half // LANES // 4)
    def _(j):
        for u in range(4):
            cols = span_of(j * 4 + u)
            far = span_of(half // LANES + j * 4 + u)
            live = valid[:, far] > 0
            values = [refl[k, :, far] for k in range(bands)]
            (b,) = packet_of(values, live, day_col, rows, packet_rows, (odd,))
            sx[:, cols] = b
            live = valid[:, cols] > 0
            values = [refl[k, :, cols] for k in range(bands)]
            (c,) = packet_of(values, live, day_col, rows, packet_rows, (odd,))
            side[:, cols] = jnp.where(inner, c, b)


def nearness(packet):
    return jnp.broadcast_to(packet[packet.shape[0] - 1 :], packet.shape)


def join_near_kernel(own, got, out):
    @pl.loop(0, own.shape[1] // LANES // 4)
    def _(j):
        for u in range(4):
            cols = span_of(j * 4 + u)
            a, b = own[:, cols], got[:, cols]
            out[:, cols] = jnp.where(nearness(a) >= nearness(b), a, b)


def join_own_kernel(own, got, out):
    _, _, inner = flags()

    @pl.loop(0, own.shape[1] // LANES // 4)
    def _(j):
        for u in range(4):
            cols = span_of(j * 4 + u)
            a, b = own[:, cols], got[:, cols]
            use = jnp.logical_and(inner, nearness(a) > 0.0)
            out[:, cols] = jnp.where(use, a, b)


def merge_first(refs, cols):
    _, upper, inner = flags()
    main, side, other = (r[:, cols] for r in refs)
    side = jnp.where(inner, 0.0, side)
    other = jnp.where(inner, other, 0.0)
    near = jnp.where(nearness(main) >= nearness(side), main, side)
    return jnp.where(upper, near, other), jnp.where(upper, other, near)


def merge_second(refs, cols):
    _, upper, inner = flags()
    main, more, side = (r[:, cols] for r in refs)
    other = jnp.where(inner, side, 0.0)
    near = jnp.where(nearness(main) >= nearness(more), main, more)
    return jnp.where(upper, near, other), jnp.where(upper, other, near)


def merge_all(bits, refs, cols):
    me = lax.axis_index("date")
    before = jnp.zeros((refs[0].shape[0], LANES), jnp.float32)
    after = before
    for t, ref in zip(bits, refs):
        got = ref[:, cols]
        prev = jnp.where(bit_of(me, t), got, 0.0)
        nxt = jnp.where(bit_of(me, t), 0.0, got)
        before = jnp.where(nearness(prev) > nearness(before), prev, before)
        after = jnp.where(nearness(nxt) > nearness(after), nxt, after)
    return before, after


def near_kernel(refl, valid, day_in, prev_out, next_out, prev_days, next_days):
    bands, count, pixels = refl.shape
    rows, _ = tile_rows(bands, count)
    day_col = day_in[...]

    @pl.loop(0, pixels // LANES // 4)
    def _(j):
        for u in range(4):
            cols = span_of(j * 4 + u)
            live = valid[:, cols] > 0
            prev_pos = running(jnp.where(live, rows, -1), rows, count, True)
            next_pos = running(jnp.where(live, rows, count), rows, count, False)
            prev_in = prev_pos >= 0
            next_in = next_pos < count
            prev_pos = prev_pos & (count - 1)
            next_pos = next_pos & (count - 1)
            prev_days[:, cols] = jnp.where(prev_in, pick(day_col, prev_pos), 0.0)
            next_days[:, cols] = jnp.where(next_in, pick(day_col, next_pos), TOP)
            for b in range(bands):
                x = refl[b, :, cols]
                prev_out[b, :, cols] = pick(x, prev_pos)
                next_out[b, :, cols] = pick(x, next_pos)


def fill_kernel(start, width, piece, packets, merge, *refs):
    prev_own, next_own, prev_days, next_days, day_in = refs[:5]
    gots = refs[5 : 5 + packets]
    out, buf, sems = refs[-3:]
    bands, _, _ = prev_own.shape
    day_col = day_in[...]
    copies = []
    for k in range(width // piece):

        @pl.loop(0, piece // LANES // 4)
        def _(j):
            for u in range(4):
                i = k * (piece // LANES) + j * 4 + u
                cols = span_of(i)
                far = span_of(start // LANES + i)
                before, after = merge(gots, cols)
                prev_day, next_day = prev_days[:, far], next_days[:, far]
                prev_in, next_in = prev_day > 0.0, next_day < TOP
                prev_day = jnp.where(prev_in, prev_day, before[bands:])
                next_day = jnp.where(next_in, next_day, TOP - after[bands:])
                has_prev = prev_day > 0.0
                both = jnp.logical_and(has_prev, next_day < TOP)
                span = jnp.maximum(jnp.where(both, next_day - prev_day, 1.0), 1.0)
                weight = jnp.where(
                    both, (day_col - prev_day) / span, jnp.where(has_prev, 0.0, 1.0)
                )
                for b in range(bands):
                    prev = jnp.where(prev_in, prev_own[b, :, far], before[b : b + 1])
                    nxt = jnp.where(next_in, next_own[b, :, far], after[b : b + 1])
                    buf[b, :, cols] = prev + weight * (nxt - prev)

        copy = pltpu.make_async_copy(
            buf.at[:, :, pl.ds(k * piece, piece)],
            out.at[:, :, pl.ds(start + k * piece, piece)],
            sems.at[k],
        )
        copy.start()
        copies.append(copy)
    for copy in copies:
        copy.wait()


def nearest(refl, valid, day_col):
    bands, count, pixels = refl.shape
    return pl.pallas_call(
        near_kernel,
        in_specs=[VMEM] * 3,
        out_specs=[VMEM] * 4,
        out_shape=[f32(bands, count, pixels)] * 2 + [f32(count, pixels)] * 2,
        compiler_params=PARAMS,
        name="nearest",
    )(refl, valid, day_col)


def fill(start, piece, merge, near, day_col, gots, out=None):
    bands, count, pixels = near[0].shape
    width = gots[0].shape[1]
    held = () if out is None else (out,)
    return pl.pallas_call(
        functools.partial(fill_kernel, start, width, piece, len(gots), merge),
        in_specs=[VMEM] * (5 + len(gots)) + [HBM] * len(held),
        out_specs=HBM,
        out_shape=f32(bands, count, pixels),
        input_output_aliases={} if out is None else {5 + len(gots): 0},
        scratch_shapes=[
            pltpu.VMEM((bands, count, width), jnp.float32),
            pltpu.SemaphoreType.DMA((width // piece,)),
        ],
        compiler_params=PARAMS,
    )(*near, day_col, *gots, *held)


def load(piece, width, bits, days, stack, validity):
    bands, count, _ = stack.shape
    args = (pltpu.with_memory_space_constraint(a, pltpu.HBM) for a in (days, stack, validity))
    return pl.pallas_call(
        functools.partial(load_kernel, piece, bits),
        in_specs=[HBM] * 3,
        out_specs=[VMEM] * (1 + len(bits)),
        out_shape=[f32(count, LANES)] + [f32(bands + 1, width)] * len(bits),
        scratch_shapes=[
            pltpu.VMEM((bands, count, width), jnp.float32),
            pltpu.VMEM((count, width), jnp.int32),
            pltpu.SMEM((count,), jnp.int32),
            pltpu.SemaphoreType.DMA,
            pltpu.SemaphoreType.DMA((2 * (width // piece + 1),)),
        ],
        compiler_params=PARAMS,
        name="load",
    )(*args)


def body_any(devices, reflectance, validity, day_number):
    pixels = reflectance.shape[2]
    piece = pixels // 8
    stack = jnp.transpose(reflectance, (1, 0, 2))
    bits = list(range((devices - 1).bit_length()))
    day_col, *sends = load(piece, pixels, bits, day_number, stack, validity)
    refl, valid = stack, validity
    gots, tops = [], []
    for k in range(1, 1 << len(bits)):
        pairs = [(d, d ^ k) for d in range(devices) if d ^ k < devices]
        tops.append(k.bit_length() - 1)
        gots.append(lax.ppermute(sends[tops[-1]], "date", pairs))
    merge = functools.partial(merge_all, tops)
    out = fill(0, piece, merge, nearest(refl, valid, day_col), day_col, gots)
    return jnp.transpose(out, (1, 0, 2))


def body(reflectance, validity, day_number):
    _, bands, pixels = reflectance.shape
    half = pixels // 2
    piece = half // 4
    stack = jnp.transpose(reflectance, (1, 0, 2))
    packet = f32(bands + 1, half)

    def across(x):
        return lax.ppermute(x, "date", [(d, d ^ 1) for d in range(4)])

    def along(x):
        return lax.ppermute(x, "date", [(d, d ^ 2) for d in range(4)])

    day_col, sy1 = load(piece, half, (1,), day_number, stack, validity)
    refl, valid = stack, validity
    got1 = across(sy1)

    def packets(kernel, results):
        return pl.pallas_call(
            kernel,
            in_specs=[VMEM] * 3,
            out_specs=[VMEM] * results,
            out_shape=[packet] * results,
            compiler_params=PARAMS,
        )(refl, valid, day_col)

    (sy2,) = packets(second_kernel, 1)
    got2 = along(sy2)
    sx2, side = packets(side_kernel, 2)
    side = across(side)
    join = dict(
        in_specs=[VMEM] * 2, out_specs=VMEM, out_shape=packet, compiler_params=PARAMS
    )
    joined1 = pl.pallas_call(join_near_kernel, name="join_first", **join)(sy1, got1)
    far1 = along(joined1)
    joined2 = pl.pallas_call(join_own_kernel, name="join_second", **join)(sx2, got2)
    far2 = across(joined2)
    arrays = (nearest(refl, valid, day_col), day_col)
    out = fill(0, piece, merge_first, *arrays, (far1, side, got1))
    out = fill(half, piece, merge_second, *arrays, (got2, far2, side), out)
    return jnp.transpose(out, (1, 0, 2))


def solution(mesh):
    placed = (P("date", None, ("tile", "pix")), P("date", ("tile", "pix")), P("date"))
    devices = mesh.shape["date"]
    return jax.shard_map(
        body if devices == 4 else functools.partial(body_any, devices),
        mesh=mesh,
        in_specs=placed,
        out_specs=P("date", None, ("tile", "pix")),
        check_vma=False,
    )
```

```python
import functools

import jax
import jax.numpy as jnp
from jax import lax
from jax.experimental import pallas as pl
from jax.experimental.pallas import tpu as pltpu
from jax.sharding import PartitionSpec as P


LANES = 128
UNROLL = 16
TOP = 1048576.0
VMEM = pl.BlockSpec(memory_space=pltpu.VMEM)
HBM = pl.BlockSpec(memory_space=pltpu.HBM)
PARAMS = pltpu.CompilerParams(vmem_limit_bytes=16 << 20)


def f32(*shape):
    return jax.ShapeDtypeStruct(shape, jnp.float32)


def pick(x, pos):
    return jnp.take_along_axis(x, pos, axis=0, mode="promise_in_bounds")


def sublane_max(x, count):
    step = 1
    while step < count:
        x = jnp.maximum(x, pltpu.roll(x, step, 0))
        step *= 2
    return x


def running(pos, rows, count, forward):
    step = 1
    while step < count:
        if forward:
            moved = pltpu.roll(pos, step, 0)
            pos = jnp.maximum(pos, jnp.where(rows >= step, moved, -1))
        else:
            moved = pltpu.roll(pos, count - step, 0)
            pos = jnp.minimum(pos, jnp.where(rows < count - step, moved, count))
        step *= 2
    return pos


def span_of(i):
    return pl.ds(pl.multiple_of(i * LANES, LANES), LANES)


def packet_of(values, live, day_col, rows, packet_rows, firsts):
    count = rows.shape[0]
    bands = len(values)
    outs = []
    for first in firsts:
        order = jnp.where(first, count - rows, rows + 1)
        best = sublane_max(jnp.where(live, order, 0), count)
        pos = jnp.where(first, count - best, best - 1) & (count - 1)
        near = jnp.where(first, TOP - day_col, day_col)
        got = pick(near, pos)
        for b in range(bands):
            got = jnp.where(packet_rows == b, pick(values[b], pos), got)
        outs.append(jnp.where(best > 0, got, 0.0))
    return outs


def bit_of(me, t):
    return lax.rem(lax.div(me, 1 << t), 2) == 1


def flags():
    me = lax.axis_index("date")
    return bit_of(me, 0), bit_of(me, 1), jnp.logical_or(me == 1, me == 2)


def tile_rows(bands, count):
    rows = lax.broadcasted_iota(jnp.int32, (count, LANES), 0)
    packet_rows = lax.broadcasted_iota(jnp.int32, (bands + 1, LANES), 0)
    return rows, packet_rows


def load_kernel(piece, bits, days_in, refl_in, valid_in, day_out, *rest):
    sends, (refl, valid, days, day_sem, sems) = rest[: len(bits)], rest[len(bits) :]
    bands, count, _ = refl.shape
    half = sends[0].shape[1]
    day_copy = pltpu.make_async_copy(days_in, days, day_sem)
    day_copy.start()
    copies = []
    at = 0
    while at < half:
        width = piece
        cols = pl.ds(at, width)
        k = len(copies)
        pair = (
            pltpu.make_async_copy(
                valid_in.at[:, cols], valid.at[:, cols], sems.at[2 * k]
            ),
            pltpu.make_async_copy(
                refl_in.at[:, :, cols], refl.at[:, :, cols], sems.at[2 * k + 1]
            ),
        )
        for c in pair:
            c.start(priority=1)
        copies.append(pair)
        at += width
    rows, packet_rows = tile_rows(bands, count)
    me = lax.axis_index("date")
    firsts = [bit_of(me, t) for t in bits]
    day_copy.wait()
    day_col = jnp.zeros((count, LANES), jnp.float32)
    for t in range(count):
        day_col = jnp.where(rows == t, days[t].astype(jnp.float32), day_col)
    day_out[...] = day_col
    for k in range(half // piece):
        for c in copies[k]:
            c.wait()

        @pl.loop(0, piece // LANES // UNROLL)
        def _(j):
            for u in range(UNROLL):
                cols = span_of(k * (piece // LANES) + j * UNROLL + u)
                live = valid[:, cols] > 0
                values = [refl[b, :, cols] for b in range(bands)]
                packets = packet_of(values, live, day_col, rows, packet_rows, firsts)
                for send, packet in zip(sends, packets):
                    send[:, cols] = packet


def second_kernel(refl, valid, day_in, sy):
    bands, count, pixels = refl.shape
    half = pixels // 2
    rows, packet_rows = tile_rows(bands, count)
    _, upper, _ = flags()
    day_col = day_in[...]

    @pl.loop(0, half // LANES // UNROLL)
    def _(j):
        for u in range(UNROLL):
            cols = span_of(j * UNROLL + u)
            far = span_of(half // LANES + j * UNROLL + u)
            live = valid[:, far] > 0
            values = [refl[k, :, far] for k in range(bands)]
            (a,) = packet_of(values, live, day_col, rows, packet_rows, (upper,))
            sy[:, cols] = a


def side_kernel(refl, valid, day_in, sx, side):
    bands, count, pixels = refl.shape
    half = pixels // 2
    rows, packet_rows = tile_rows(bands, count)
    odd, _, inner = flags()
    day_col = day_in[...]

    @pl.loop(0, half // LANES // UNROLL)
    def _(j):
        for u in range(UNROLL):
            cols = span_of(j * UNROLL + u)
            far = span_of(half // LANES + j * UNROLL + u)
            live = valid[:, far] > 0
            values = [refl[k, :, far] for k in range(bands)]
            (b,) = packet_of(values, live, day_col, rows, packet_rows, (odd,))
            sx[:, cols] = b
            live = valid[:, cols] > 0
            values = [refl[k, :, cols] for k in range(bands)]
            (c,) = packet_of(values, live, day_col, rows, packet_rows, (odd,))
            side[:, cols] = jnp.where(inner, c, b)


def nearness(packet):
    return jnp.broadcast_to(packet[packet.shape[0] - 1 :], packet.shape)


def join_near_kernel(own, got, out):
    @pl.loop(0, own.shape[1] // LANES // UNROLL)
    def _(j):
        for u in range(UNROLL):
            cols = span_of(j * UNROLL + u)
            a, b = own[:, cols], got[:, cols]
            out[:, cols] = jnp.where(nearness(a) >= nearness(b), a, b)


def join_own_kernel(own, got, out):
    _, _, inner = flags()

    @pl.loop(0, own.shape[1] // LANES // UNROLL)
    def _(j):
        for u in range(UNROLL):
            cols = span_of(j * UNROLL + u)
            a, b = own[:, cols], got[:, cols]
            use = jnp.logical_and(inner, nearness(a) > 0.0)
            out[:, cols] = jnp.where(use, a, b)


def merge_first(refs, cols):
    _, upper, inner = flags()
    main, side, other = (r[:, cols] for r in refs)
    side = jnp.where(inner, 0.0, side)
    other = jnp.where(inner, other, 0.0)
    near = jnp.where(nearness(main) >= nearness(side), main, side)
    return jnp.where(upper, near, other), jnp.where(upper, other, near)


def merge_second(refs, cols):
    _, upper, inner = flags()
    main, more, side = (r[:, cols] for r in refs)
    other = jnp.where(inner, side, 0.0)
    near = jnp.where(nearness(main) >= nearness(more), main, more)
    return jnp.where(upper, near, other), jnp.where(upper, other, near)


def merge_all(bits, refs, cols):
    me = lax.axis_index("date")
    before = jnp.zeros((refs[0].shape[0], LANES), jnp.float32)
    after = before
    for t, ref in zip(bits, refs):
        got = ref[:, cols]
        prev = jnp.where(bit_of(me, t), got, 0.0)
        nxt = jnp.where(bit_of(me, t), 0.0, got)
        before = jnp.where(nearness(prev) > nearness(before), prev, before)
        after = jnp.where(nearness(nxt) > nearness(after), nxt, after)
    return before, after


def near_kernel(refl, valid, day_in, prev_out, next_out, prev_days, next_days):
    bands, count, pixels = refl.shape
    rows, _ = tile_rows(bands, count)
    day_col = day_in[...]

    @pl.loop(0, pixels // LANES // UNROLL)
    def _(j):
        for u in range(UNROLL):
            cols = span_of(j * UNROLL + u)
            live = valid[:, cols] > 0
            prev_pos = running(jnp.where(live, rows, -1), rows, count, True)
            next_pos = running(jnp.where(live, rows, count), rows, count, False)
            prev_in = prev_pos >= 0
            next_in = next_pos < count
            prev_pos = prev_pos & (count - 1)
            next_pos = next_pos & (count - 1)
            prev_days[:, cols] = jnp.where(prev_in, pick(day_col, prev_pos), 0.0)
            next_days[:, cols] = jnp.where(next_in, pick(day_col, next_pos), TOP)
            for b in range(bands):
                x = refl[b, :, cols]
                prev_out[b, :, cols] = pick(x, prev_pos)
                next_out[b, :, cols] = pick(x, next_pos)


def fill_kernel(start, width, piece, packets, merge, *refs):
    prev_own, next_own, prev_days, next_days, day_in = refs[:5]
    gots = refs[5 : 5 + packets]
    out, buf, sems = refs[-3:]
    bands, _, _ = prev_own.shape
    day_col = day_in[...]
    copies = []
    for k in range(width // piece):

        @pl.loop(0, piece // LANES // 8)
        def _(j):
            for u in range(8):
                i = k * (piece // LANES) + j * 8 + u
                cols = span_of(i)
                far = span_of(start // LANES + i)
                before, after = merge(gots, cols)
                prev_day, next_day = prev_days[:, far], next_days[:, far]
                prev_in, next_in = prev_day > 0.0, next_day < TOP
                prev_day = jnp.where(prev_in, prev_day, before[bands:])
                next_day = jnp.where(next_in, next_day, TOP - after[bands:])
                has_prev = prev_day > 0.0
                both = jnp.logical_and(has_prev, next_day < TOP)
                span = jnp.maximum(jnp.where(both, next_day - prev_day, 1.0), 1.0)
                weight = jnp.where(
                    both, (day_col - prev_day) / span, jnp.where(has_prev, 0.0, 1.0)
                )
                for b in range(bands):
                    prev = jnp.where(prev_in, prev_own[b, :, far], before[b : b + 1])
                    nxt = jnp.where(next_in, next_own[b, :, far], after[b : b + 1])
                    buf[b, :, cols] = prev + weight * (nxt - prev)

        copy = pltpu.make_async_copy(
            buf.at[:, :, pl.ds(k * piece, piece)],
            out.at[:, :, pl.ds(start + k * piece, piece)],
            sems.at[k],
        )
        copy.start()
        copies.append(copy)
    for copy in copies:
        copy.wait()


def nearest(refl, valid, day_col):
    bands, count, pixels = refl.shape
    return pl.pallas_call(
        near_kernel,
        in_specs=[VMEM] * 3,
        out_specs=[VMEM] * 4,
        out_shape=[f32(bands, count, pixels)] * 2 + [f32(count, pixels)] * 2,
        compiler_params=PARAMS,
        name="nearest",
    )(refl, valid, day_col)


def fill(start, piece, merge, near, day_col, gots, out=None):
    bands, count, pixels = near[0].shape
    width = gots[0].shape[1]
    held = () if out is None else (out,)
    return pl.pallas_call(
        functools.partial(fill_kernel, start, width, piece, len(gots), merge),
        in_specs=[VMEM] * (5 + len(gots)) + [HBM] * len(held),
        out_specs=HBM,
        out_shape=f32(bands, count, pixels),
        input_output_aliases={} if out is None else {5 + len(gots): 0},
        scratch_shapes=[
            pltpu.VMEM((bands, count, width), jnp.float32),
            pltpu.SemaphoreType.DMA((width // piece,)),
        ],
        compiler_params=PARAMS,
    )(*near, day_col, *gots, *held)


def load(piece, width, bits, days, stack, validity):
    bands, count, _ = stack.shape
    args = (pltpu.with_memory_space_constraint(a, pltpu.HBM) for a in (days, stack, validity))
    return pl.pallas_call(
        functools.partial(load_kernel, piece, bits),
        in_specs=[HBM] * 3,
        out_specs=[VMEM] * (1 + len(bits)),
        out_shape=[f32(count, LANES)] + [f32(bands + 1, width)] * len(bits),
        scratch_shapes=[
            pltpu.VMEM((bands, count, width), jnp.float32),
            pltpu.VMEM((count, width), jnp.int32),
            pltpu.SMEM((count,), jnp.int32),
            pltpu.SemaphoreType.DMA,
            pltpu.SemaphoreType.DMA((2 * (width // piece + 1),)),
        ],
        compiler_params=PARAMS,
        name="load",
    )(*args)


def body_any(devices, reflectance, validity, day_number):
    pixels = reflectance.shape[2]
    piece = pixels // 4
    stack = jnp.transpose(reflectance, (1, 0, 2))
    bits = list(range((devices - 1).bit_length()))
    day_col, *sends = load(piece, pixels, bits, day_number, stack, validity)
    refl, valid = stack, validity
    gots, tops = [], []
    for k in range(1, 1 << len(bits)):
        pairs = [(d, d ^ k) for d in range(devices) if d ^ k < devices]
        tops.append(k.bit_length() - 1)
        gots.append(lax.ppermute(sends[tops[-1]], "date", pairs))
    merge = functools.partial(merge_all, tops)
    out = fill(0, piece, merge, nearest(refl, valid, day_col), day_col, gots)
    return jnp.transpose(out, (1, 0, 2))


def body(reflectance, validity, day_number):
    _, bands, pixels = reflectance.shape
    half = pixels // 2
    piece = half // 4
    stack = jnp.transpose(reflectance, (1, 0, 2))
    packet = f32(bands + 1, half)

    def across(x):
        return lax.ppermute(x, "date", [(d, d ^ 1) for d in range(4)])

    def along(x):
        return lax.ppermute(x, "date", [(d, d ^ 2) for d in range(4)])

    day_col, sy1 = load(half // 2, half, (1,), day_number, stack, validity)
    refl, valid = stack, validity
    got1 = across(sy1)

    def packets(kernel, results):
        return pl.pallas_call(
            kernel,
            in_specs=[VMEM] * 3,
            out_specs=[VMEM] * results,
            out_shape=[packet] * results,
            compiler_params=PARAMS,
        )(refl, valid, day_col)

    (sy2,) = packets(second_kernel, 1)
    got2 = along(sy2)
    sx2, side = packets(side_kernel, 2)
    side = across(side)
    join = dict(
        in_specs=[VMEM] * 2, out_specs=VMEM, out_shape=packet, compiler_params=PARAMS
    )
    joined1 = pl.pallas_call(join_near_kernel, name="join_first", **join)(sy1, got1)
    far1 = along(joined1)
    joined2 = pl.pallas_call(join_own_kernel, name="join_second", **join)(sx2, got2)
    far2 = across(joined2)
    arrays = (nearest(refl, valid, day_col), day_col)
    out = fill(0, piece, merge_first, *arrays, (far1, side, got1))
    out = fill(half, piece, merge_second, *arrays, (got2, far2, side), out)
    return jnp.transpose(out, (1, 0, 2))


def solution(mesh):
    placed = (P("date", None, ("tile", "pix")), P("date", ("tile", "pix")), P("date"))
    devices = mesh.shape["date"]
    return jax.shard_map(
        body if devices == 4 else functools.partial(body_any, devices),
        mesh=mesh,
        in_specs=placed,
        out_specs=P("date", None, ("tile", "pix")),
        check_vma=False,
    )
```

```python
import functools

import jax
import jax.numpy as jnp
from jax import lax
from jax.experimental import pallas as pl
from jax.experimental.pallas import tpu as pltpu
from jax.sharding import PartitionSpec as P


LANES = 128
UNROLL = 16
TOP = 1048576.0
VMEM = pl.BlockSpec(memory_space=pltpu.VMEM)
HBM = pl.BlockSpec(memory_space=pltpu.HBM)
PARAMS = pltpu.CompilerParams(vmem_limit_bytes=16 << 20)


def f32(*shape):
    return jax.ShapeDtypeStruct(shape, jnp.float32)


def pick(x, pos):
    return jnp.take_along_axis(x, pos, axis=0, mode="promise_in_bounds")


def sublane_max(x, count):
    step = 1
    while step < count:
        x = jnp.maximum(x, pltpu.roll(x, step, 0))
        step *= 2
    return x


def running(pos, rows, count, forward):
    step = 1
    while step < count:
        if forward:
            moved = pltpu.roll(pos, step, 0)
            pos = jnp.maximum(pos, jnp.where(rows >= step, moved, -1))
        else:
            moved = pltpu.roll(pos, count - step, 0)
            pos = jnp.minimum(pos, jnp.where(rows < count - step, moved, count))
        step *= 2
    return pos


def span_of(i):
    return pl.ds(pl.multiple_of(i * LANES, LANES), LANES)


def each_tile(tiles, most=UNROLL):
    def run(work):
        if tiles == 0:
            return
        step = max(u for u in range(1, most + 1) if tiles % u == 0)

        @pl.loop(0, tiles // step)
        def _(j):
            for u in range(step):
                work(j * step + u)

    return run


def packet_of(values, live, day_col, rows, packet_rows, firsts):
    count = rows.shape[0]
    bands = len(values)
    outs = []
    for first in firsts:
        order = jnp.where(first, count - rows, rows + 1)
        best = sublane_max(jnp.where(live, order, 0), count)
        pos = jnp.where(first, count - best, best - 1) & (count - 1)
        near = jnp.where(first, TOP - day_col, day_col)
        got = pick(near, pos)
        for b in range(bands):
            got = jnp.where(packet_rows == b, pick(values[b], pos), got)
        outs.append(jnp.where(best > 0, got, 0.0))
    return outs


def bit_of(me, t):
    return lax.rem(lax.div(me, 1 << t), 2) == 1


def flags():
    me = lax.axis_index("date")
    return bit_of(me, 0), bit_of(me, 1), jnp.logical_or(me == 1, me == 2)


def tile_rows(bands, count):
    rows = lax.broadcasted_iota(jnp.int32, (count, LANES), 0)
    packet_rows = lax.broadcasted_iota(jnp.int32, (bands + 1, LANES), 0)
    return rows, packet_rows


def load_kernel(piece, bits, days_in, refl_in, valid_in, day_out, *rest):
    sends, (refl, valid, days, day_sem, sems) = rest[: len(bits)], rest[len(bits) :]
    bands, count, _ = refl.shape
    half = sends[0].shape[1]
    day_copy = pltpu.make_async_copy(days_in, days, day_sem)
    day_copy.start()
    copies = []
    at = 0
    while at < half:
        width = piece
        cols = pl.ds(at, width)
        k = len(copies)
        pair = (
            pltpu.make_async_copy(
                valid_in.at[:, cols], valid.at[:, cols], sems.at[2 * k]
            ),
            pltpu.make_async_copy(
                refl_in.at[:, :, cols], refl.at[:, :, cols], sems.at[2 * k + 1]
            ),
        )
        for c in pair:
            c.start(priority=1)
        copies.append(pair)
        at += width
    rows, packet_rows = tile_rows(bands, count)
    me = lax.axis_index("date")
    firsts = [bit_of(me, t) for t in bits]
    day_copy.wait()
    day_col = jnp.zeros((count, LANES), jnp.float32)
    for t in range(count):
        day_col = jnp.where(rows == t, days[t].astype(jnp.float32), day_col)
    day_out[...] = day_col
    for k in range(half // piece):
        for c in copies[k]:
            c.wait()

        @each_tile(piece // LANES)
        def _(i):
            cols = span_of(k * (piece // LANES) + i)
            live = valid[:, cols] > 0
            values = [refl[b, :, cols] for b in range(bands)]
            packets = packet_of(values, live, day_col, rows, packet_rows, firsts)
            for send, packet in zip(sends, packets):
                send[:, cols] = packet


def second_kernel(refl, valid, day_in, sy):
    bands, count, pixels = refl.shape
    tiles = sy.shape[1] // LANES
    rows, packet_rows = tile_rows(bands, count)
    _, upper, _ = flags()
    day_col = day_in[...]

    @each_tile(tiles)
    def _(i):
        cols = span_of(i)
        far = span_of(pixels // LANES - tiles + i)
        live = valid[:, far] > 0
        values = [refl[k, :, far] for k in range(bands)]
        (a,) = packet_of(values, live, day_col, rows, packet_rows, (upper,))
        sy[:, cols] = a


def side_kernel(refl, valid, day_in, sx, side):
    bands, count, pixels = refl.shape
    seconds = sx.shape[1] // LANES
    firsts = pixels // LANES - seconds
    rows, packet_rows = tile_rows(bands, count)
    odd, _, inner = flags()
    day_col = day_in[...]

    def made(cols):
        live = valid[:, cols] > 0
        values = [refl[k, :, cols] for k in range(bands)]
        return packet_of(values, live, day_col, rows, packet_rows, (odd,))[0]

    @each_tile(min(firsts, seconds))
    def _(i):
        cols = span_of(i)
        far = made(span_of(firsts + i))
        sx[:, cols] = far
        side[:, cols] = jnp.where(inner, made(cols), far)

    @each_tile(abs(firsts - seconds))
    def _(i):
        cols = span_of(min(firsts, seconds) + i)
        if firsts > seconds:
            side[:, cols] = made(cols)
        else:
            far = made(span_of(firsts + firsts + i))
            sx[:, cols] = far
            side[:, cols] = far


def nearness(packet):
    return jnp.broadcast_to(packet[packet.shape[0] - 1 :], packet.shape)


def join_near_kernel(own, got, out):
    @each_tile(own.shape[1] // LANES)
    def _(i):
        cols = span_of(i)
        a, b = own[:, cols], got[:, cols]
        out[:, cols] = jnp.where(nearness(a) >= nearness(b), a, b)


def join_own_kernel(own, got, out):
    _, _, inner = flags()

    @each_tile(own.shape[1] // LANES)
    def _(i):
        cols = span_of(i)
        a, b = own[:, cols], got[:, cols]
        use = jnp.logical_and(inner, nearness(a) > 0.0)
        out[:, cols] = jnp.where(use, a, b)


def merge_first(refs, cols):
    _, upper, inner = flags()
    main, side, other = (r[:, cols] for r in refs)
    side = jnp.where(inner, 0.0, side)
    other = jnp.where(inner, other, 0.0)
    near = jnp.where(nearness(main) >= nearness(side), main, side)
    return jnp.where(upper, near, other), jnp.where(upper, other, near)


def merge_second(refs, cols):
    _, upper, inner = flags()
    main, more, side = (r[:, cols] for r in refs)
    other = jnp.where(inner, side, 0.0)
    near = jnp.where(nearness(main) >= nearness(more), main, more)
    return jnp.where(upper, near, other), jnp.where(upper, other, near)


def merge_all(bits, refs, cols):
    me = lax.axis_index("date")
    before = jnp.zeros((refs[0].shape[0], LANES), jnp.float32)
    after = before
    for t, ref in zip(bits, refs):
        got = ref[:, cols]
        prev = jnp.where(bit_of(me, t), got, 0.0)
        nxt = jnp.where(bit_of(me, t), 0.0, got)
        before = jnp.where(nearness(prev) > nearness(before), prev, before)
        after = jnp.where(nearness(nxt) > nearness(after), nxt, after)
    return before, after


def near_kernel(refl, valid, day_in, prev_out, next_out, prev_days, next_days):
    bands, count, pixels = refl.shape
    rows, _ = tile_rows(bands, count)
    day_col = day_in[...]

    @each_tile(pixels // LANES)
    def _(i):
        cols = span_of(i)
        live = valid[:, cols] > 0
        prev_pos = running(jnp.where(live, rows, -1), rows, count, True)
        next_pos = running(jnp.where(live, rows, count), rows, count, False)
        prev_in = prev_pos >= 0
        next_in = next_pos < count
        prev_pos = prev_pos & (count - 1)
        next_pos = next_pos & (count - 1)
        prev_days[:, cols] = jnp.where(prev_in, pick(day_col, prev_pos), 0.0)
        next_days[:, cols] = jnp.where(next_in, pick(day_col, next_pos), TOP)
        for b in range(bands):
            x = refl[b, :, cols]
            prev_out[b, :, cols] = pick(x, prev_pos)
            next_out[b, :, cols] = pick(x, next_pos)


def fill_kernel(start, width, piece, packets, merge, *refs):
    prev_own, next_own, prev_days, next_days, day_in = refs[:5]
    gots = refs[5 : 5 + packets]
    out, buf, sems = refs[-3:]
    bands, _, _ = prev_own.shape
    day_col = day_in[...]
    copies = []
    for k in range(width // piece):

        @each_tile(piece // LANES, 10)
        def _(i):
            i = k * (piece // LANES) + i
            cols = span_of(i)
            far = span_of(start // LANES + i)
            before, after = merge(gots, cols)
            prev_day, next_day = prev_days[:, far], next_days[:, far]
            prev_in, next_in = prev_day > 0.0, next_day < TOP
            prev_day = jnp.where(prev_in, prev_day, before[bands:])
            next_day = jnp.where(next_in, next_day, TOP - after[bands:])
            has_prev = prev_day > 0.0
            both = jnp.logical_and(has_prev, next_day < TOP)
            span = jnp.maximum(jnp.where(both, next_day - prev_day, 1.0), 1.0)
            weight = jnp.where(
                both, (day_col - prev_day) / span, jnp.where(has_prev, 0.0, 1.0)
            )
            for b in range(bands):
                prev = jnp.where(prev_in, prev_own[b, :, far], before[b : b + 1])
                nxt = jnp.where(next_in, next_own[b, :, far], after[b : b + 1])
                buf[b, :, cols] = prev + weight * (nxt - prev)

        copy = pltpu.make_async_copy(
            buf.at[:, :, pl.ds(k * piece, piece)],
            out.at[:, :, pl.ds(start + k * piece, piece)],
            sems.at[k],
        )
        copy.start()
        copies.append(copy)
    for copy in copies:
        copy.wait()


def nearest(refl, valid, day_col):
    bands, count, pixels = refl.shape
    return pl.pallas_call(
        near_kernel,
        in_specs=[VMEM] * 3,
        out_specs=[VMEM] * 4,
        out_shape=[f32(bands, count, pixels)] * 2 + [f32(count, pixels)] * 2,
        compiler_params=PARAMS,
        name="nearest",
    )(refl, valid, day_col)


def fill(start, piece, merge, near, day_col, gots, out=None):
    bands, count, pixels = near[0].shape
    width = gots[0].shape[1]
    held = () if out is None else (out,)
    return pl.pallas_call(
        functools.partial(fill_kernel, start, width, piece, len(gots), merge),
        in_specs=[VMEM] * (5 + len(gots)) + [HBM] * len(held),
        out_specs=HBM,
        out_shape=f32(bands, count, pixels),
        input_output_aliases={} if out is None else {5 + len(gots): 0},
        scratch_shapes=[
            pltpu.VMEM((bands, count, width), jnp.float32),
            pltpu.SemaphoreType.DMA((width // piece,)),
        ],
        compiler_params=PARAMS,
    )(*near, day_col, *gots, *held)


def load(piece, width, bits, days, stack, validity):
    bands, count, _ = stack.shape
    args = (pltpu.with_memory_space_constraint(a, pltpu.HBM) for a in (days, stack, validity))
    return pl.pallas_call(
        functools.partial(load_kernel, piece, bits),
        in_specs=[HBM] * 3,
        out_specs=[VMEM] * (1 + len(bits)),
        out_shape=[f32(count, LANES)] + [f32(bands + 1, width)] * len(bits),
        scratch_shapes=[
            pltpu.VMEM((bands, count, width), jnp.float32),
            pltpu.VMEM((count, width), jnp.int32),
            pltpu.SMEM((count,), jnp.int32),
            pltpu.SemaphoreType.DMA,
            pltpu.SemaphoreType.DMA((2 * (width // piece + 1),)),
        ],
        compiler_params=PARAMS,
        name="load",
    )(*args)


def pieces_of(width, most):
    return width // max(n for n in range(1, most + 1) if width % (n * LANES) == 0)


def body_any(devices, reflectance, validity, day_number):
    pixels = reflectance.shape[2]
    piece = pixels // 4
    stack = jnp.transpose(reflectance, (1, 0, 2))
    bits = list(range((devices - 1).bit_length()))
    day_col, *sends = load(piece, pixels, bits, day_number, stack, validity)
    refl, valid = stack, validity
    gots, tops = [], []
    for k in range(1, 1 << len(bits)):
        pairs = [(d, d ^ k) for d in range(devices) if d ^ k < devices]
        tops.append(k.bit_length() - 1)
        gots.append(lax.ppermute(sends[tops[-1]], "date", pairs))
    merge = functools.partial(merge_all, tops)
    out = fill(0, piece, merge, nearest(refl, valid, day_col), day_col, gots)
    return jnp.transpose(out, (1, 0, 2))


def body(reflectance, validity, day_number):
    _, bands, pixels = reflectance.shape
    first = pixels // LANES * 8 // 16 * LANES
    second = pixels - first
    stack = jnp.transpose(reflectance, (1, 0, 2))

    def across(x):
        return lax.ppermute(x, "date", [(d, d ^ 1) for d in range(4)])

    def along(x):
        return lax.ppermute(x, "date", [(d, d ^ 2) for d in range(4)])

    day_col, sy1 = load(pieces_of(first, 2), first, (1,), day_number, stack, validity)
    refl, valid = stack, validity
    got1 = across(sy1)

    def packets(kernel, widths):
        return pl.pallas_call(
            kernel,
            in_specs=[VMEM] * 3,
            out_specs=[VMEM] * len(widths),
            out_shape=[f32(bands + 1, w) for w in widths],
            compiler_params=PARAMS,
        )(refl, valid, day_col)

    (sy2,) = packets(second_kernel, [second])
    got2 = along(sy2)
    sx2, side = packets(side_kernel, [second, max(first, second)])
    side = across(side)

    def join(kernel, own, got):
        return pl.pallas_call(
            kernel,
            in_specs=[VMEM] * 2,
            out_specs=VMEM,
            out_shape=f32(*own.shape),
            compiler_params=PARAMS,
        )(own, got)

    far1 = along(join(join_near_kernel, sy1, got1))
    far2 = across(join(join_own_kernel, sx2, got2))
    arrays = (nearest(refl, valid, day_col), day_col)
    piece = pieces_of(first, 4)
    out = fill(0, piece, merge_first, *arrays, (far1, side, got1))
    piece = pieces_of(second, 4)
    out = fill(first, piece, merge_second, *arrays, (got2, far2, side), out)
    return jnp.transpose(out, (1, 0, 2))


def solution(mesh):
    placed = (P("date", None, ("tile", "pix")), P("date", ("tile", "pix")), P("date"))
    devices = mesh.shape["date"]
    return jax.shard_map(
        body if devices == 4 else functools.partial(body_any, devices),
        mesh=mesh,
        in_specs=placed,
        out_specs=P("date", None, ("tile", "pix")),
        check_vma=False,
    )
```

```python
import functools

import jax
import jax.numpy as jnp
from jax import lax
from jax.experimental import pallas as pl
from jax.experimental.pallas import tpu as pltpu
from jax.sharding import PartitionSpec as P


LANES = 128
UNROLL = 16
TOP = 1048576.0
VMEM = pl.BlockSpec(memory_space=pltpu.VMEM)
HBM = pl.BlockSpec(memory_space=pltpu.HBM)
PARAMS = pltpu.CompilerParams(vmem_limit_bytes=16 << 20)


def f32(*shape):
    return jax.ShapeDtypeStruct(shape, jnp.float32)


def pick(x, pos):
    return jnp.take_along_axis(x, pos, axis=0, mode="promise_in_bounds")


def sublane_max(x, count):
    step = 1
    while step < count:
        x = jnp.maximum(x, pltpu.roll(x, step, 0))
        step *= 2
    return x


def running(pos, rows, count, forward):
    step = 1
    while step < count:
        if forward:
            moved = pltpu.roll(pos, step, 0)
            pos = jnp.maximum(pos, jnp.where(rows >= step, moved, -1))
        else:
            moved = pltpu.roll(pos, count - step, 0)
            pos = jnp.minimum(pos, jnp.where(rows < count - step, moved, count))
        step *= 2
    return pos


def span_of(i):
    return pl.ds(pl.multiple_of(i * LANES, LANES), LANES)


def each_tile(tiles, most=UNROLL):
    def run(work):
        if tiles == 0:
            return
        step = max(u for u in range(1, most + 1) if tiles % u == 0)

        @pl.loop(0, tiles // step)
        def _(j):
            for u in range(step):
                work(j * step + u)

    return run


def packet_of(values, live, day_col, rows, packet_rows, firsts):
    count = rows.shape[0]
    bands = len(values)
    outs = []
    for first in firsts:
        order = jnp.where(first, count - rows, rows + 1)
        best = sublane_max(jnp.where(live, order, 0), count)
        pos = jnp.where(first, count - best, best - 1) & (count - 1)
        near = jnp.where(first, TOP - day_col, day_col)
        got = pick(near, pos)
        for b in range(bands):
            got = jnp.where(packet_rows == b, pick(values[b], pos), got)
        outs.append(jnp.where(best > 0, got, 0.0))
    return outs


def bit_of(me, t):
    return lax.rem(lax.div(me, 1 << t), 2) == 1


def flags():
    me = lax.axis_index("date")
    return bit_of(me, 0), bit_of(me, 1), jnp.logical_or(me == 1, me == 2)


def tile_rows(bands, count):
    rows = lax.broadcasted_iota(jnp.int32, (count, LANES), 0)
    packet_rows = lax.broadcasted_iota(jnp.int32, (bands + 1, LANES), 0)
    return rows, packet_rows


def load_kernel(piece, bits, days_in, refl_in, valid_in, day_out, *rest):
    sends, (refl, valid, days, day_sem, sems) = rest[: len(bits)], rest[len(bits) :]
    bands, count, _ = refl.shape
    half = sends[0].shape[1]
    day_copy = pltpu.make_async_copy(days_in, days, day_sem)
    copies = []
    at = 0
    while at < half:
        width = piece
        cols = pl.ds(at, width)
        k = len(copies)
        pair = (
            pltpu.make_async_copy(
                valid_in.at[:, cols], valid.at[:, cols], sems.at[2 * k]
            ),
            pltpu.make_async_copy(
                refl_in.at[:, :, cols], refl.at[:, :, cols], sems.at[2 * k + 1]
            ),
        )
        for c in pair:
            c.start(priority=1)
        copies.append(pair)
        at += width
    day_copy.start()
    rows, packet_rows = tile_rows(bands, count)
    me = lax.axis_index("date")
    firsts = [bit_of(me, t) for t in bits]
    day_copy.wait()
    day_col = jnp.zeros((count, LANES), jnp.float32)
    for t in range(count):
        day_col = jnp.where(rows == t, days[t].astype(jnp.float32), day_col)
    day_out[...] = day_col
    for k in range(half // piece):
        for c in copies[k]:
            c.wait()

        @each_tile(piece // LANES)
        def _(i):
            cols = span_of(k * (piece // LANES) + i)
            live = valid[:, cols] > 0
            values = [refl[b, :, cols] for b in range(bands)]
            packets = packet_of(values, live, day_col, rows, packet_rows, firsts)
            for send, packet in zip(sends, packets):
                send[:, cols] = packet


def second_kernel(refl, valid, day_in, sy):
    bands, count, pixels = refl.shape
    tiles = sy.shape[1] // LANES
    rows, packet_rows = tile_rows(bands, count)
    _, upper, _ = flags()
    day_col = day_in[...]

    @each_tile(tiles)
    def _(i):
        cols = span_of(i)
        far = span_of(pixels // LANES - tiles + i)
        live = valid[:, far] > 0
        values = [refl[k, :, far] for k in range(bands)]
        (a,) = packet_of(values, live, day_col, rows, packet_rows, (upper,))
        sy[:, cols] = a


def side_kernel(refl, valid, day_in, sx, side):
    bands, count, pixels = refl.shape
    seconds = sx.shape[1] // LANES
    firsts = pixels // LANES - seconds
    rows, packet_rows = tile_rows(bands, count)
    odd, _, inner = flags()
    day_col = day_in[...]

    turns = jnp.where(lax.rem(lax.axis_index("tile"), 2) == 1, 60, 0)
    spun = lax.fori_loop(0, turns, lambda i, v: v * 1.0001 + 0.5, day_col)
    day_col = jnp.where(spun < 0.0, spun, day_col)

    def made(cols):
        live = valid[:, cols] > 0
        values = [refl[k, :, cols] for k in range(bands)]
        return packet_of(values, live, day_col, rows, packet_rows, (odd,))[0]

    @each_tile(min(firsts, seconds))
    def _(i):
        cols = span_of(i)
        far = made(span_of(firsts + i))
        sx[:, cols] = far
        side[:, cols] = jnp.where(inner, made(cols), far)

    @each_tile(abs(firsts - seconds))
    def _(i):
        cols = span_of(min(firsts, seconds) + i)
        if firsts > seconds:
            side[:, cols] = made(cols)
        else:
            far = made(span_of(firsts + firsts + i))
            sx[:, cols] = far
            side[:, cols] = far


def nearness(packet):
    return jnp.broadcast_to(packet[packet.shape[0] - 1 :], packet.shape)


def join_near_kernel(own, got, out):
    @each_tile(own.shape[1] // LANES)
    def _(i):
        cols = span_of(i)
        a, b = own[:, cols], got[:, cols]
        out[:, cols] = jnp.where(nearness(a) >= nearness(b), a, b)


def join_own_kernel(own, got, out):
    _, _, inner = flags()

    @each_tile(own.shape[1] // LANES)
    def _(i):
        cols = span_of(i)
        a, b = own[:, cols], got[:, cols]
        use = jnp.logical_and(inner, nearness(a) > 0.0)
        out[:, cols] = jnp.where(use, a, b)


def merge_first(refs, cols):
    _, upper, inner = flags()
    main, side, other = (r[:, cols] for r in refs)
    side = jnp.where(inner, 0.0, side)
    other = jnp.where(inner, other, 0.0)
    near = jnp.where(nearness(main) >= nearness(side), main, side)
    return jnp.where(upper, near, other), jnp.where(upper, other, near)


def merge_second(refs, cols):
    _, upper, inner = flags()
    main, more, side = (r[:, cols] for r in refs)
    other = jnp.where(inner, side, 0.0)
    near = jnp.where(nearness(main) >= nearness(more), main, more)
    return jnp.where(upper, near, other), jnp.where(upper, other, near)


def merge_all(bits, refs, cols):
    me = lax.axis_index("date")
    before = jnp.zeros((refs[0].shape[0], LANES), jnp.float32)
    after = before
    for t, ref in zip(bits, refs):
        got = ref[:, cols]
        prev = jnp.where(bit_of(me, t), got, 0.0)
        nxt = jnp.where(bit_of(me, t), 0.0, got)
        before = jnp.where(nearness(prev) > nearness(before), prev, before)
        after = jnp.where(nearness(nxt) > nearness(after), nxt, after)
    return before, after


def near_kernel(refl, valid, day_in, prev_out, next_out, prev_days, next_days):
    bands, count, pixels = refl.shape
    rows, _ = tile_rows(bands, count)
    day_col = day_in[...]

    @each_tile(pixels // LANES, 4)
    def _(i):
        cols = span_of(i)
        live = valid[:, cols] > 0
        prev_pos = running(jnp.where(live, rows, -1), rows, count, True)
        next_pos = running(jnp.where(live, rows, count), rows, count, False)
        prev_in = prev_pos >= 0
        next_in = next_pos < count
        prev_pos = prev_pos & (count - 1)
        next_pos = next_pos & (count - 1)
        prev_days[:, cols] = jnp.where(prev_in, pick(day_col, prev_pos), 0.0)
        next_days[:, cols] = jnp.where(next_in, pick(day_col, next_pos), TOP)
        for b in range(bands):
            x = refl[b, :, cols]
            prev_out[b, :, cols] = pick(x, prev_pos)
            next_out[b, :, cols] = pick(x, next_pos)


def fill_kernel(start, width, piece, packets, merge, *refs):
    prev_own, next_own, prev_days, next_days, day_in = refs[:5]
    gots = refs[5 : 5 + packets]
    out, buf, sems = refs[-3:]
    bands, _, _ = prev_own.shape
    day_col = day_in[...]
    copies = []
    for k in range(width // piece):

        @each_tile(piece // LANES, 10)
        def _(i):
            i = k * (piece // LANES) + i
            cols = span_of(i)
            far = span_of(start // LANES + i)
            before, after = merge(gots, cols)
            prev_day, next_day = prev_days[:, far], next_days[:, far]
            prev_in, next_in = prev_day > 0.0, next_day < TOP
            prev_day = jnp.where(prev_in, prev_day, before[bands:])
            next_day = jnp.where(next_in, next_day, TOP - after[bands:])
            has_prev = prev_day > 0.0
            both = jnp.logical_and(has_prev, next_day < TOP)
            span = jnp.maximum(jnp.where(both, next_day - prev_day, 1.0), 1.0)
            weight = jnp.where(
                both, (day_col - prev_day) / span, jnp.where(has_prev, 0.0, 1.0)
            )
            for b in range(bands):
                prev = jnp.where(prev_in, prev_own[b, :, far], before[b : b + 1])
                nxt = jnp.where(next_in, next_own[b, :, far], after[b : b + 1])
                buf[b, :, cols] = prev + weight * (nxt - prev)

        copy = pltpu.make_async_copy(
            buf.at[:, :, pl.ds(k * piece, piece)],
            out.at[:, :, pl.ds(start + k * piece, piece)],
            sems.at[k],
        )
        copy.start()
        copies.append(copy)
    for copy in copies:
        copy.wait()


def nearest(refl, valid, day_col):
    bands, count, pixels = refl.shape
    return pl.pallas_call(
        near_kernel,
        in_specs=[VMEM] * 3,
        out_specs=[VMEM] * 4,
        out_shape=[f32(bands, count, pixels)] * 2 + [f32(count, pixels)] * 2,
        compiler_params=PARAMS,
        name="nearest",
    )(refl, valid, day_col)


def fill(start, piece, merge, near, day_col, gots, out=None):
    bands, count, pixels = near[0].shape
    width = gots[0].shape[1]
    held = () if out is None else (out,)
    return pl.pallas_call(
        functools.partial(fill_kernel, start, width, piece, len(gots), merge),
        in_specs=[VMEM] * (5 + len(gots)) + [HBM] * len(held),
        out_specs=HBM,
        out_shape=f32(bands, count, pixels),
        input_output_aliases={} if out is None else {5 + len(gots): 0},
        scratch_shapes=[
            pltpu.VMEM((bands, count, width), jnp.float32),
            pltpu.SemaphoreType.DMA((width // piece,)),
        ],
        compiler_params=PARAMS,
    )(*near, day_col, *gots, *held)


def load(piece, width, bits, days, stack, validity):
    bands, count, _ = stack.shape
    args = (pltpu.with_memory_space_constraint(a, pltpu.HBM) for a in (days, stack, validity))
    return pl.pallas_call(
        functools.partial(load_kernel, piece, bits),
        in_specs=[HBM] * 3,
        out_specs=[VMEM] * (1 + len(bits)),
        out_shape=[f32(count, LANES)] + [f32(bands + 1, width)] * len(bits),
        scratch_shapes=[
            pltpu.VMEM((bands, count, width), jnp.float32),
            pltpu.VMEM((count, width), jnp.int32),
            pltpu.SMEM((count,), jnp.int32),
            pltpu.SemaphoreType.DMA,
            pltpu.SemaphoreType.DMA((2 * (width // piece + 1),)),
        ],
        compiler_params=PARAMS,
        name="load",
    )(*args)


def pieces_of(width, most):
    return width // max(n for n in range(1, most + 1) if width % (n * LANES) == 0)


def body_any(devices, reflectance, validity, day_number):
    pixels = reflectance.shape[2]
    piece = pixels // 4
    stack = jnp.transpose(reflectance, (1, 0, 2))
    bits = list(range((devices - 1).bit_length()))
    day_col, *sends = load(piece, pixels, bits, day_number, stack, validity)
    refl, valid = stack, validity
    gots, tops = [], []
    for k in range(1, 1 << len(bits)):
        pairs = [(d, d ^ k) for d in range(devices) if d ^ k < devices]
        tops.append(k.bit_length() - 1)
        gots.append(lax.ppermute(sends[tops[-1]], "date", pairs))
    merge = functools.partial(merge_all, tops)
    out = fill(0, piece, merge, nearest(refl, valid, day_col), day_col, gots)
    return jnp.transpose(out, (1, 0, 2))


def body(reflectance, validity, day_number):
    _, bands, pixels = reflectance.shape
    first = pixels // LANES * 8 // 16 * LANES
    second = pixels - first
    stack = jnp.transpose(reflectance, (1, 0, 2))

    def across(x):
        return lax.ppermute(x, "date", [(d, d ^ 1) for d in range(4)])

    def along(x):
        return lax.ppermute(x, "date", [(d, d ^ 2) for d in range(4)])

    day_col, sy1 = load(pieces_of(first, 2), first, (1,), day_number, stack, validity)
    refl, valid = stack, validity
    got1 = across(sy1)

    def packets(kernel, widths):
        return pl.pallas_call(
            kernel,
            in_specs=[VMEM] * 3,
            out_specs=[VMEM] * len(widths),
            out_shape=[f32(bands + 1, w) for w in widths],
            compiler_params=PARAMS,
        )(refl, valid, day_col)

    (sy2,) = packets(second_kernel, [second])
    got2 = along(sy2)
    sx2, side = packets(side_kernel, [second, max(first, second)])
    side = across(side)

    def join(kernel, own, got):
        return pl.pallas_call(
            kernel,
            in_specs=[VMEM] * 2,
            out_specs=VMEM,
            out_shape=f32(*own.shape),
            compiler_params=PARAMS,
        )(own, got)

    far1 = along(join(join_near_kernel, sy1, got1))
    far2 = across(join(join_own_kernel, sx2, got2))
    arrays = (nearest(refl, valid, day_col), day_col)
    piece = pieces_of(first, 4)
    out = fill(0, piece, merge_first, *arrays, (far1, side, got1))
    piece = pieces_of(second, 4)
    out = fill(first, piece, merge_second, *arrays, (got2, far2, side), out)
    return jnp.transpose(out, (1, 0, 2))


def solution(mesh):
    placed = (P("date", None, ("tile", "pix")), P("date", ("tile", "pix")), P("date"))
    devices = mesh.shape["date"]
    return jax.shard_map(
        body if devices == 4 else functools.partial(body_any, devices),
        mesh=mesh,
        in_specs=placed,
        out_specs=P("date", None, ("tile", "pix")),
        check_vma=False,
    )
```
